32 devices in a mesh: energy: 2 (over y), slab: 16 (over z, x, core).
Axes of the slice: x: 2, y: 2, z: 4, core: 2. Of those that a mesh axis runs over, the one named last changes fastest.
Arguments:
- slab_green: bfloat16 [2, 128, 128, 128], P(None, ('energy', 'slab')), parts along dimension 1, may hold values from -1 to 1, as said below
- coupling: bfloat16 [2, 128, 128, 128], P(None, ('energy', 'slab')), parts along dimension 1, may hold values from -40 to 40
- left_lead_surface: bfloat16 [4, 128, 128], P('energy'), parts along dimension 0, may hold values from -8 to 8, as said below
- sigma_right: bfloat16 [4, 128, 128], P('energy'), parts along dimension 0, may hold values from -120 to 120, as said below
Outputs:
- green_diagonal: float32 [2, 128, 128, 128], P(None, ('energy', 'slab')), parts along dimension 1
The draws below stay inside these ranges and needn't reach their ends.
There are 2 independent parts, one for each index of `energy`. The reference program is written for one: setup_inputs(seed, part) draws one part's arguments, and reference() takes and returns one part's arrays. A program takes and returns all parts, laid end to end along the dimension named above; each array names one. Nothing has to cross between parts.
Inputs may be any that keep to these rules, and one draw needn't show every extreme that they name: Each block of slab_green, both parts, equals its own transpose. `left_lead_surface`: both parts equal their own transposes. `sigma_right`: both parts equal their own transposes.
All inputs are finite; a program needn't handle non-finite values.
Results may differ from the reference program's by a relative error of at most 0.035.
Values may be sent and summed in bfloat16 or wider, within the bound.
A program may use at most 128 MiB of HBM per device.

```python
import math
import jax
import jax.numpy as jnp
from jax import lax

W = 128
WIRE_LAYERS = 64


slab_scale = 0.1


def channel_draw(key):
    base = jax.random.fold_in(key, 7)
    divided_seeds = jax.random.split(base, 8)
    fraction = jax.random.uniform(divided_seeds[0], (W,), minval=0.0, maxval=1.0)
    lowest, highest = (0.7, 1.4)
    slowest = 10.0 ** (-0.3 / WIRE_LAYERS)
    fastest = 0.45
    damping_widths = fastest ** (1.0 - fraction) * slowest ** fraction
    spike_samples = jnp.where(jax.random.randint(divided_seeds[1], (WIRE_LAYERS,), 0, WIRE_LAYERS) < 3, 0.85, 1.0)
    damping_widths = damping_widths[None, :] * spike_samples[:, None]
    magnitude = jnp.exp(jax.random.uniform(divided_seeds[2], (WIRE_LAYERS, W), minval=math.log(lowest), maxval=math.log(highest)))
    first_phase = jax.random.uniform(divided_seeds[3], (WIRE_LAYERS, W), minval=-math.pi, maxval=math.pi)
    second_phase = jax.random.uniform(divided_seeds[4], (WIRE_LAYERS, W), minval=-math.pi, maxval=math.pi)
    return (damping_widths, magnitude, first_phase, second_phase, divided_seeds)


def symmetric_noise(key, shape):
    noise = jnp.clip(jax.random.normal(key, shape, jnp.float32), -5.0, 5.0)
    return (noise + jnp.swapaxes(noise, -1, -2)) / math.sqrt(2.0)


def draw_slab_green(key, part):
    damping_widths, magnitude, first_phase, second_phase, divided_seeds = channel_draw(key)
    square = jnp.eye(W, dtype=jnp.float32)
    hermitian_principal = slab_scale * magnitude * jnp.cos(first_phase)
    imag_diag = slab_scale * magnitude * jnp.sin(first_phase)
    diagonal = jnp.stack([hermitian_principal[:, None, :] * square, imag_diag[:, None, :] * square])
    noise = symmetric_noise(divided_seeds[5], (2, WIRE_LAYERS, W, W)) * (0.14 / math.sqrt(W)) * slab_scale
    return (diagonal + noise).astype(jnp.bfloat16)


def draw_coupling(key, part):
    damping_widths, magnitude, first_phase, second_phase, divided_seeds = channel_draw(key)
    square = jnp.eye(W, dtype=jnp.float32)
    total_amount = damping_widths / magnitude / slab_scale
    hermitian_principal = total_amount * jnp.cos(second_phase)
    imag_diag = total_amount * jnp.sin(second_phase)
    diagonal = jnp.stack([hermitian_principal[:, None, :] * square, imag_diag[:, None, :] * square])
    noise = jnp.clip(jax.random.normal(divided_seeds[6], (2, WIRE_LAYERS, W, W), jnp.float32), -5.0, 5.0)
    noise = noise * (0.11 / math.sqrt(W)) / slab_scale
    return (diagonal + noise).astype(jnp.bfloat16)


def lead_block(key, factor):
    divided_seeds = jax.random.split(key, 3)
    magnitude = jnp.exp(jax.random.uniform(divided_seeds[0], (W,), minval=math.log(0.5), maxval=math.log(2.0)))
    phase = jax.random.uniform(divided_seeds[1], (W,), minval=-math.pi, maxval=math.pi)
    square = jnp.eye(W, dtype=jnp.float32)
    diagonal = jnp.stack([(magnitude * jnp.cos(phase))[None, :] * square, (magnitude * jnp.sin(phase))[None, :] * square])
    noise = symmetric_noise(divided_seeds[2], (2, W, W)) * (0.14 / math.sqrt(W))
    return (factor * (diagonal + noise)).astype(jnp.bfloat16)


def draw_left_lead_surface(key, part):
    return lead_block(jax.random.fold_in(key, 31), 3.0)


def draw_sigma_right(key, part):
    return lead_block(jax.random.fold_in(key, 37), 30.0)


def setup_inputs(seed: int = 0, part: int = 0) -> dict:
    streams_of = jax.random.split(jax.random.key(seed), 5)
    own_keys = jax.random.split(jax.random.fold_in(streams_of[4], part), 5)
    return {
        "slab_green": draw_slab_green(jax.random.fold_in(jax.random.fold_in(streams_of[4], part), 71), part),
        "coupling": draw_coupling(jax.random.fold_in(jax.random.fold_in(streams_of[4], part), 71), part),
        "left_lead_surface": draw_left_lead_surface(jax.random.fold_in(jax.random.fold_in(streams_of[4], part), 71), part),
        "sigma_right": draw_sigma_right(jax.random.fold_in(jax.random.fold_in(streams_of[4], part), 71), part),
    }


def complex_product(left, right):
    real_part = jnp.dot(left[0], right[0], preferred_element_type=jnp.float32) - jnp.dot(left[1], right[1], preferred_element_type=jnp.float32)
    imag_part = jnp.dot(left[0], right[1], preferred_element_type=jnp.float32) + jnp.dot(left[1], right[0], preferred_element_type=jnp.float32)
    return jnp.stack([real_part, imag_part])


def times_transpose(left, right):
    random_numbers = (((1,), (1,)), ((), ()))
    real_part = lax.dot_general(left[0], right[0], random_numbers, preferred_element_type=jnp.float32) - lax.dot_general(left[1], right[1], random_numbers, preferred_element_type=jnp.float32)
    imag_part = lax.dot_general(left[0], right[1], random_numbers, preferred_element_type=jnp.float32) + lax.dot_general(left[1], right[0], random_numbers, preferred_element_type=jnp.float32)
    return jnp.stack([real_part, imag_part])


def sandwich(factor, current):
    inner = complex_product(factor, current.astype(jnp.bfloat16)).astype(jnp.bfloat16)
    return times_transpose(inner, factor)


def reference(slab_green, coupling, left_lead_surface, sigma_right):
    greens = jnp.moveaxis(slab_green, 1, 0)
    links = jnp.moveaxis(coupling, 1, 0)
    follow = jnp.concatenate([links[1:], links[:1]], axis=0)
    position = jnp.arange(WIRE_LAYERS, dtype=jnp.int32)

    def forward_step(current, element):
        block, link = element
        factor = times_transpose(block, link).astype(jnp.bfloat16)
        updated = sandwich(factor, current) + block.astype(jnp.float32)
        return updated, updated

    def backward_step(current, element):
        block, link, place = element
        factor = jnp.where(place == WIRE_LAYERS - 1, block, complex_product(block, link).astype(jnp.bfloat16))
        updated = sandwich(factor, current) + block.astype(jnp.float32)
        return updated, updated

    unused, left_connected = lax.scan(forward_step, left_lead_surface.astype(jnp.float32), (greens, links))
    unused2, right_connected = lax.scan(backward_step, sigma_right.astype(jnp.float32), (greens, follow, position), reverse=True)
    result = left_connected + right_connected - greens.astype(jnp.float32)
    return jnp.moveaxis(result, 0, 1)
```

```python
import functools

import jax
import jax.numpy as jnp
from jax import lax
from jax.experimental import pallas as pl
from jax.experimental.pallas import tpu as pltpu
from jax.sharding import PartitionSpec as P

MESH = pl.DeviceIdType.MESH
BF = jnp.bfloat16
F32 = jnp.float32


def wide(value):
    return jnp.concatenate([value[0], value[1]], axis=1)


def halves(out):
    width = out.shape[1] // 2
    return out[:, :width], out[:, width:]


def low(value):
    return value[0].astype(BF), value[1].astype(BF)


def plus(a, b):
    return a[0] + b[0], a[1] + b[1]


def times(rows, right):
    weights = jnp.concatenate(
        [wide(right), jnp.concatenate([-right[1], right[0]], axis=1)], axis=0
    )
    return jnp.dot(rows, weights, preferred_element_type=F32)


def times_transpose(rows, right):
    weights = jnp.concatenate(
        [
            jnp.concatenate([right[0], -right[1]], axis=1),
            jnp.concatenate([right[1], right[0]], axis=1),
        ],
        axis=0,
    )
    return lax.dot_general(rows, weights, (((1,), (1,)), ((), ())), preferred_element_type=F32)


def product(a, b):
    return low(halves(times(wide(a), b)))


def sandwich(factor, middle):
    inner = times(wide(factor), low(middle)).astype(BF)
    return halves(times_transpose(inner, factor))


def get(ref, *index):
    return ref[(*index, 0)], ref[(*index, 1)]


def put(ref, value, *index):
    ref[(*index, 0)] = value[0].astype(ref.dtype)
    ref[(*index, 1)] = value[1].astype(ref.dtype)


def kernel(
    bits,
    near,
    green_hbm,
    link_hbm,
    lead_hbm,
    sigma_hbm,
    out,
    green,
    link,
    lead,
    sigma,
    own,
    pair,
    given,
    factors,
    base,
    mine,
    slots,
    relay,
    inbox,
    ends,
    post,
    late,
    send_sem,
    recv_sem,
    load_sem,
):
    loads = [
        pltpu.make_async_copy(source, target, load_sem.at[k])
        for k, (source, target) in enumerate(
            [(green_hbm, green), (link_hbm, link), (lead_hbm, lead), (sigma_hbm, sigma)]
        )
    ]
    for load in loads:
        load.start()
    layers, width = green.shape[1], green.shape[2]
    energy, me = lax.axis_index("energy"), lax.axis_index("slab")
    role, chip = me % 2, me // 2
    mate = me + 1 - 2 * role
    chips, half, group = 2**bits, 2 ** (bits - 1), 2**near
    place = chip + role * (chips - 1 - 2 * chip)
    stride = (1 - 2 * role) * 2
    spot = place % group
    head = place == 0
    middle = range(near, bits - 1)
    lows = {k: place // 2 ** (k + 1) * 2 ** (k + 1) for k in middle}
    gives = {k: place == lows[k] + 2**k - 1 for k in middle}
    takes = {k: (place // 2**k) % 2 == 1 for k in middle}
    gives_last = place == half - 1
    upper = chip // half
    giver = jnp.where(upper == 1, 2 * (half - 1), 2 * half + 1)
    slow = (1 - upper + role) % 2

    barrier = pltpu.get_barrier_semaphore()

    def greet(other):
        pl.semaphore_signal(barrier, inc=1, device_id=(energy, other), device_id_type=MESH)

    greet(mate)
    expected = 1 + (group - 1 - spot)
    for d in range(1, group):

        @pl.when(spot >= d)
        def _():
            greet(me - stride * d)

    for k in middle:
        expected = expected + jnp.where(gives[k], 2**k, 0)

        @pl.when(takes[k])
        def _():
            greet(me + stride * (lows[k] + 2**k - 1 - place))

    expected = expected + jnp.where(gives_last, 2 * half, 0)
    greet_last = jnp.logical_not(giver == me)

    @pl.when(greet_last)
    def _():
        greet(giver)

    def remote(source, target, other, sender, receiver):
        return pltpu.make_async_remote_copy(
            src_ref=source,
            dst_ref=target,
            send_sem=send_sem.at[sender],
            recv_sem=recv_sem.at[receiver],
            device_id=(energy, other),
            device_id_type=MESH,
        )

    row = lax.broadcasted_iota(jnp.int32, (width, width), 0)
    column = lax.broadcasted_iota(jnp.int32, (width, width), 1)
    zeros = jnp.zeros((width, width), BF)
    square = jnp.where(row == column, 1.0, 0.0).astype(BF)
    none = (zeros, zeros)
    linear, constant = pl.ds(0, 2 * width), pl.ds(2 * width, width + 16)

    def wider(value):
        return value[0].astype(F32), value[1].astype(F32)

    def pick(test, a, b):
        return jnp.where(test, a[0], b[0]), jnp.where(test, a[1], b[1])

    def put_linear(ref, value, *index):
        ref[(*index, pl.ds(0, width))] = value[0]
        ref[(*index, pl.ds(width, width))] = value[1]

    def put_packed(ref, value, at, *index):
        ref[(*index, pl.ds(at, width))] = jnp.where(row <= column, value[0], value[1]).astype(BF)
        diagonal = jnp.sum(jnp.where(row == column, value[1], 0.0), axis=0, keepdims=True)
        ref[(*index, pl.ds(at + width, 16))] = jnp.broadcast_to(diagonal, (16, width)).astype(BF)

    def get_packed(ref, at, *index):
        mixed = ref[(*index, pl.ds(at, width))]
        flipped = mixed.T.astype(F32)
        mixed = mixed.astype(F32)
        diagonal = ref[(*index, pl.ds(at + width, 16))].astype(F32)[0:1]
        return (
            jnp.where(row <= column, mixed, flipped),
            jnp.where(row > column, mixed, jnp.where(row == column, diagonal, flipped)),
        )

    def get_map(ref, *index):
        first = (ref[(*index, pl.ds(0, width))], ref[(*index, pl.ds(width, width))])
        return first, get_packed(ref, 2 * width, *index)

    def put_map(ref, value, *index):
        put_linear(ref, value[0], *index)
        put_packed(ref, value[1], 2 * width, *index)

    blank = jnp.zeros((width + 16, width), BF)
    for d in range(1, group):

        @pl.when(spot < d)
        def _():
            put_linear(slots, (square, zeros), d - 1)
            slots[d - 1, constant] = blank

        @pl.when(place == d)
        def _():
            put_linear(slots, none, d - 1)

    for k in middle:

        @pl.when(jnp.logical_not(takes[k]))
        def _():
            put_linear(inbox, (square, zeros), k - near)
            inbox[k - near, constant] = blank

        @pl.when(jnp.logical_and(takes[k], lows[k] == 0))
        def _():
            put_linear(inbox, none, k - near)

    for load in loads[:2]:
        load.wait()

    def merged(first, second):
        return (
            product(second[0], first[0]),
            plus(sandwich(second[0], first[1]), second[1]),
        )

    def whole(items):
        while len(items) > 1:
            rest = items[len(items) // 2 * 2 :]
            items = [merged(*items[k : k + 2]) for k in range(0, len(items) - 1, 2)] + rest
        return items[0]

    def blocks():
        return (
            [(green[0, i], green[1, i]) for i in range(layers)],
            [(link[0, i], link[1, i]) for i in range(layers)],
        )

    def upward():
        g, c = blocks()
        return [(low(halves(times_transpose(wide(g[i]), c[i]))), g[i]) for i in range(layers)]

    def downward():
        g, c = blocks()
        back = [product(c[i], g[i]) for i in range(layers)]
        return [(back[i], halves(times_transpose(wide(back[i]), c[i]))) for i in range(layers)]

    def total_to(at, up):
        def _():
            value = whole(upward()) if up else whole(downward()[::-1])
            put(own, value[0], at, 0)
            put(own, value[1], at, 1)

        return _

    pl.when(role == 0)(total_to(1, False))
    pl.when(role == 1)(total_to(1, True))
    pl.semaphore_wait(barrier, expected)
    swap = remote(own.at[1], pair, mate, 0, 0)
    swap.start()
    pl.when(role == 0)(total_to(0, True))
    pl.when(role == 1)(total_to(0, False))
    hint = remote(own.at[0], given, mate, 1, 1)
    hint.start()

    for load in loads[2:]:
        load.wait()
    forward = role == 0
    start = (
        jnp.where(forward, lead[0], sigma[0]),
        jnp.where(forward, lead[1], sigma[1]),
    )
    first = (get(own, 0, 0), wider(get(own, 0, 1)))
    first = (first[0], pick(head, plus(sandwich(first[0], start), first[1]), first[1]))
    swap.wait_recv()
    total = merged(first, (get(pair, 0), wider(get(pair, 1))))
    total = (pick(head, none, total[0]), total[1])
    put_map(mine, total)

    def neighbour(d, whole_map):
        part = pl.ds(0, 3 * width + 16) if whole_map else constant
        return remote(mine.at[part], slots.at[d - 1, part], me + stride * d, 2 + d, 2 + d)

    def for_kinds(d, sender, act):
        test = spot + d < group if sender else spot >= d
        at_head = head if sender else place == d
        pl.when(jnp.logical_and(test, at_head))(lambda: act(neighbour(d, False)))
        pl.when(jnp.logical_and(test, jnp.logical_not(at_head)))(lambda: act(neighbour(d, True)))

    for d in reversed(range(1, group)):
        for_kinds(d, True, lambda copy: copy.start())

    g = blocks()[0]
    up, down = upward(), downward()[::-1]
    up_part, down_part = [up[0]], [down[0]]
    for i in range(1, layers):
        up_part.append(merged(up_part[-1], up[i]))
        if i + 1 < layers:
            down_part.append(merged(down_part[-1], down[i]))
    for i in range(layers):
        m_part, s_part = up_part[i]
        put(factors, m_part, role, i)
        if i + 1 < layers:
            m_rest, s_rest = down_part[layers - 2 - i]
            put(factors, product(g[i], m_rest), 1 - role, i)
            put(base, plus(s_part, sandwich(g[i], s_rest)), i)
        else:
            put(factors, g[i], 1 - role, i)
            put(base, s_part, i)
    hint.wait_recv()
    for i in range(layers):
        factor = get(factors, 1, i)
        put(base, plus(get(base, i), sandwich(factor, get(given, 1))), i)
        put(factors, product(factor, get(given, 0)), 1, i)

    for d in reversed(range(1, group)):
        for_kinds(d, False, lambda copy: copy.wait_recv())
    arrived = [get_map(slots, d - 1) for d in reversed(range(1, group))]
    if arrived:
        lower = arrived[:-1] and [whole(arrived[:-1])]
        before = whole(lower + arrived[-1:])
        total = whole(lower + [merged(arrived[-1], total)])
    else:
        before = ((square, zeros), wider(none))
    before = (pick(head, none, before[0]), pick(head, wider(start), before[1]))

    def deliveries(k, whole_map):
        part = pl.ds(0, 3 * width + 16) if whole_map else constant
        at = 2 + group + 2 ** k - 2**near
        return [
            remote(relay.at[k - near, part], inbox.at[k - near, part], me + stride * (1 + d), at + d, 2 + group + k - near)
            for d in range(2**k)
        ]

    for k in middle:

        @pl.when(gives[k])
        def _():
            put_map(relay, total, k - near)

        for whole_map in (False, True):

            @pl.when(jnp.logical_and(gives[k], (lows[k] != 0) == whole_map))
            def _():
                for copy in reversed(deliveries(k, whole_map)):
                    copy.start()

            @pl.when(jnp.logical_and(takes[k], (lows[k] != 0) == whole_map))
            def _():
                deliveries(k, whole_map)[0].wait_recv()

        got = get_map(inbox, k - near)
        total = merged(got, total)
        before = merged(got, before)

    last = 2 + group + half - 2**near
    last_recv = 2 + group + len(middle)

    def final(d, twin):
        other = me + stride * (1 + d)
        other = other + 1 - 2 * role if twin else other
        return remote(post, late, other, last + 2 * d + twin, last_recv)

    @pl.when(gives_last)
    def _():
        put_packed(post, total[1], 0)
        for d in reversed(range(half)):
            final(d, 0).start()
            final(d, 1).start()

    put(ends, before[0], 0, 0)
    put(ends, before[1], 0, 1)
    share = remote(ends.at[0], ends.at[1], mate, 2, 2)
    share.start()

    def add(k):
        rows = jnp.concatenate([wide(get(factors, k, i)) for i in range(layers)], axis=0)
        inner = times(rows, get(ends, k, 1)).astype(BF)
        for i in range(layers):
            term = halves(times_transpose(inner[i * width : (i + 1) * width], get(factors, k, i)))
            put(base, plus(get(base, i), term), i)

    add(0)
    share.wait_recv()
    add(1)
    edge = get(ends, slow, 0)
    rows = jnp.concatenate([wide(get(factors, slow, i)) for i in range(layers)], axis=0)
    rows = times(rows, edge).astype(BF)
    final(0, 0).wait_recv()
    state = low(get_packed(late, 0))
    inner = times(rows, state).astype(BF)
    for i in range(layers):
        part = slice(i * width, (i + 1) * width)
        value = plus(get(base, i), halves(times_transpose(inner[part], halves(rows[part]))))
        out[0, i] = value[0]
        out[1, i] = value[1]

    swap.wait_send()
    hint.wait_send()
    share.wait_send()
    for d in range(1, group):
        for_kinds(d, True, lambda copy: copy.wait_send())
    for k in middle:
        for whole_map in (False, True):

            @pl.when(jnp.logical_and(gives[k], (lows[k] != 0) == whole_map))
            def _():
                for copy in deliveries(k, whole_map):
                    copy.wait_send()

    @pl.when(gives_last)
    def _():
        for d in range(half):
            final(d, 0).wait_send()
            final(d, 1).wait_send()


def solution(mesh):
    peers = mesh.shape["slab"]
    bits = (peers // 2).bit_length() - 1
    near = min(2, bits - 1)
    group, half, hops = 2**near, 2 ** (bits - 1), bits - 1 - near

    def local(slab_green, coupling, left_lead_surface, sigma_right):
        layers, width = slab_green.shape[1], slab_green.shape[2]
        vmem = pl.BlockSpec(memory_space=pltpu.VMEM)
        block = (2, width, width)
        packed, chart = (width + 16, width), (3 * width + 16, width)
        return pl.pallas_call(
            functools.partial(kernel, bits, near),
            out_shape=jax.ShapeDtypeStruct(slab_green.shape, F32),
            in_specs=[pl.BlockSpec(memory_space=pltpu.HBM)] * 4,
            out_specs=vmem,
            scratch_shapes=[
                pltpu.VMEM(slab_green.shape, BF),
                pltpu.VMEM(coupling.shape, BF),
                pltpu.VMEM(block, BF),
                pltpu.VMEM(block, BF),
                pltpu.VMEM((2, 2, *block), BF),
                pltpu.VMEM((2, *block), BF),
                pltpu.VMEM((2, *block), BF),
                pltpu.VMEM((2, layers, *block), BF),
                pltpu.VMEM((layers, *block), F32),
                pltpu.VMEM(chart, BF),
                pltpu.VMEM((max(group - 1, 1), *chart), BF),
                pltpu.VMEM((max(hops, 1), *chart), BF),
                pltpu.VMEM((max(hops, 1), *chart), BF),
                pltpu.VMEM((2, 2, *block), BF),
                pltpu.VMEM(packed, BF),
                pltpu.VMEM(packed, BF),
                pltpu.SemaphoreType.DMA((2 + group + half - group + 2 * half,)),
                pltpu.SemaphoreType.DMA((3 + group + hops,)),
                pltpu.SemaphoreType.DMA((4,)),
            ],
            compiler_params=pltpu.CompilerParams(collective_id=0, has_side_effects=True, vmem_limit_bytes=16777216),
        )(*[pltpu.with_memory_space_constraint(a, pltpu.HBM) for a in (slab_green, coupling, left_lead_surface, sigma_right)])

    in_specs = (
        P(None, ("energy", "slab"), None, None),
        P(None, ("energy", "slab"), None, None),
        P("energy", None, None),
        P("energy", None, None),
    )
    out_specs = P(None, ("energy", "slab"), None, None)
    return jax.shard_map(local, mesh=mesh, in_specs=in_specs, out_specs=out_specs, check_vma=False)
```

```python
import functools

import jax
import jax.numpy as jnp
from jax import lax
from jax.experimental import pallas as pl
from jax.experimental.pallas import tpu as pltpu
from jax.sharding import PartitionSpec as P

MESH = pl.DeviceIdType.MESH
BF = jnp.bfloat16
F32 = jnp.float32


def wide(value):
    return jnp.concatenate([value[0], value[1]], axis=1)


def halves(out):
    width = out.shape[1] // 2
    return out[:, :width], out[:, width:]


def low(value):
    return value[0].astype(BF), value[1].astype(BF)


def plus(a, b):
    return a[0] + b[0], a[1] + b[1]


def times(rows, right):
    weights = jnp.concatenate(
        [wide(right), jnp.concatenate([-right[1], right[0]], axis=1)], axis=0
    )
    return jnp.dot(rows, weights, preferred_element_type=F32)


def times_transpose(rows, right):
    weights = jnp.concatenate(
        [
            jnp.concatenate([right[0], -right[1]], axis=1),
            jnp.concatenate([right[1], right[0]], axis=1),
        ],
        axis=0,
    )
    return lax.dot_general(rows, weights, (((1,), (1,)), ((), ())), preferred_element_type=F32)


def product(a, b):
    return low(halves(times(wide(a), b)))


def sandwich(factor, middle):
    inner = times(wide(factor), low(middle)).astype(BF)
    return halves(times_transpose(inner, factor))


def get(ref, *index):
    return ref[(*index, 0)], ref[(*index, 1)]


def put(ref, value, *index):
    ref[(*index, 0)] = value[0].astype(ref.dtype)
    ref[(*index, 1)] = value[1].astype(ref.dtype)


def kernel(
    bits,
    near,
    green_hbm,
    link_hbm,
    lead_hbm,
    sigma_hbm,
    out,
    green,
    link,
    lead,
    sigma,
    own,
    pair,
    given,
    factors,
    base,
    mine,
    slots,
    relay,
    inbox,
    ends,
    post,
    late,
    send_sem,
    recv_sem,
    load_sem,
    met,
):
    loads = [
        pltpu.make_async_copy(source, target, load_sem.at[k])
        for k, (source, target) in enumerate(
            [(green_hbm, green), (link_hbm, link), (lead_hbm, lead), (sigma_hbm, sigma)]
        )
    ]
    for load in loads:
        load.start()
    layers, width = green.shape[1], green.shape[2]
    energy, me = lax.axis_index("energy"), lax.axis_index("slab")
    role, chip = me % 2, me // 2
    mate = me + 1 - 2 * role
    chips, half, group = 2**bits, 2 ** (bits - 1), 2**near
    place = chip + role * (chips - 1 - 2 * chip)
    stride = (1 - 2 * role) * 2
    spot = place % group
    head = place == 0
    middle = range(near, bits - 1)
    lows = {k: place // 2 ** (k + 1) * 2 ** (k + 1) for k in middle}
    gives = {k: place == lows[k] + 2**k - 1 for k in middle}
    takes = {k: (place // 2**k) % 2 == 1 for k in middle}
    gives_last = place == half - 1
    upper = chip // half
    giver = jnp.where(upper == 1, 2 * (half - 1), 2 * half + 1)
    slow = (1 - upper + role) % 2

    barrier = pltpu.get_barrier_semaphore()

    def greet(other):
        pl.semaphore_signal(barrier, inc=1, device_id=(energy, other), device_id_type=MESH)

    def far_greet(other):
        greet(other // 2 * 2 + 1)

    def receivers(place):
        found = group - 1 - place % group + jnp.where(place == half - 1, 2 * half, 0)
        for k in middle:
            found = found + jnp.where(place % 2 ** (k + 1) == 2**k - 1, 2**k, 0)
        return found

    for d in range(1, group):

        @pl.when(spot >= d)
        def _():
            far_greet(me - stride * d)

    for k in middle:

        @pl.when(takes[k])
        def _():
            far_greet(me + stride * (lows[k] + 2**k - 1 - place))

    far_greet(giver)

    def tell(at):
        pl.semaphore_signal(met.at[at], inc=1, device_id=(energy, mate), device_id_type=MESH)

    @pl.when(role == 1)
    def _():
        greet(mate)

    @pl.when(role == 0)
    def _():
        pl.semaphore_wait(barrier, 1)
        tell(0)

    def remote(source, target, other, sender, receiver):
        return pltpu.make_async_remote_copy(
            src_ref=source,
            dst_ref=target,
            send_sem=send_sem.at[sender],
            recv_sem=recv_sem.at[receiver],
            device_id=(energy, other),
            device_id_type=MESH,
        )

    row = lax.broadcasted_iota(jnp.int32, (width, width), 0)
    column = lax.broadcasted_iota(jnp.int32, (width, width), 1)
    zeros = jnp.zeros((width, width), BF)
    square = jnp.where(row == column, 1.0, 0.0).astype(BF)
    none = (zeros, zeros)
    linear, constant = pl.ds(0, 2 * width), pl.ds(2 * width, width + 16)

    def wider(value):
        return value[0].astype(F32), value[1].astype(F32)

    def pick(test, a, b):
        return jnp.where(test, a[0], b[0]), jnp.where(test, a[1], b[1])

    def put_linear(ref, value, *index):
        ref[(*index, pl.ds(0, width))] = value[0]
        ref[(*index, pl.ds(width, width))] = value[1]

    def put_packed(ref, value, at, *index):
        ref[(*index, pl.ds(at, width))] = jnp.where(row <= column, value[0], value[1]).astype(BF)
        diagonal = jnp.sum(jnp.where(row == column, value[1], 0.0), axis=0, keepdims=True)
        ref[(*index, pl.ds(at + width, 16))] = jnp.broadcast_to(diagonal, (16, width)).astype(BF)

    def get_packed(ref, at, *index):
        mixed = ref[(*index, pl.ds(at, width))]
        flipped = mixed.T.astype(F32)
        mixed = mixed.astype(F32)
        diagonal = ref[(*index, pl.ds(at + width, 16))].astype(F32)[0:1]
        return (
            jnp.where(row <= column, mixed, flipped),
            jnp.where(row > column, mixed, jnp.where(row == column, diagonal, flipped)),
        )

    def get_map(ref, *index):
        first = (ref[(*index, pl.ds(0, width))], ref[(*index, pl.ds(width, width))])
        return first, get_packed(ref, 2 * width, *index)

    def put_map(ref, value, *index):
        put_linear(ref, value[0], *index)
        put_packed(ref, value[1], 2 * width, *index)

    blank = jnp.zeros((width + 16, width), BF)
    for d in range(1, group):

        @pl.when(spot < d)
        def _():
            put_linear(slots, (square, zeros), d - 1)
            slots[d - 1, constant] = blank

        @pl.when(place == d)
        def _():
            put_linear(slots, none, d - 1)

    for k in middle:

        @pl.when(jnp.logical_not(takes[k]))
        def _():
            put_linear(inbox, (square, zeros), k - near)
            inbox[k - near, constant] = blank

        @pl.when(jnp.logical_and(takes[k], lows[k] == 0))
        def _():
            put_linear(inbox, none, k - near)

    for load in loads[:2]:
        load.wait()

    def merged(first, second):
        return (
            product(second[0], first[0]),
            plus(sandwich(second[0], first[1]), second[1]),
        )

    def whole(items):
        while len(items) > 1:
            rest = items[len(items) // 2 * 2 :]
            items = [merged(*items[k : k + 2]) for k in range(0, len(items) - 1, 2)] + rest
        return items[0]

    def blocks():
        return (
            [(green[0, i], green[1, i]) for i in range(layers)],
            [(link[0, i], link[1, i]) for i in range(layers)],
        )

    def upward():
        g, c = blocks()
        return [(low(halves(times_transpose(wide(g[i]), c[i]))), g[i]) for i in range(layers)]

    def downward():
        g, c = blocks()
        back = [product(c[i], g[i]) for i in range(layers)]
        return [(back[i], halves(times_transpose(wide(back[i]), c[i]))) for i in range(layers)]

    def total_to(at, up):
        def _():
            value = whole(upward()) if up else whole(downward()[::-1])
            put(own, value[0], at, 0)
            put(own, value[1], at, 1)

        return _

    pl.when(role == 0)(total_to(1, False))
    pl.when(role == 1)(total_to(1, True))

    @pl.when(role == 1)
    def _():
        pl.semaphore_wait(met.at[0], 1)

    swap = remote(own.at[1], pair, mate, 0, 0)
    swap.start()
    pl.when(role == 0)(total_to(0, True))
    pl.when(role == 1)(total_to(0, False))
    hint = remote(own.at[0], given, mate, 1, 1)
    hint.start()

    for load in loads[2:]:
        load.wait()
    forward = role == 0
    start = (
        jnp.where(forward, lead[0], sigma[0]),
        jnp.where(forward, lead[1], sigma[1]),
    )
    first = (get(own, 0, 0), wider(get(own, 0, 1)))
    first = (first[0], pick(head, plus(sandwich(first[0], start), first[1]), first[1]))
    swap.wait_recv()

    @pl.when(role == 1)
    def _():
        pl.semaphore_wait(barrier, receivers(chip) + receivers(chips - 1 - chip))
        tell(1)

    total = merged(first, (get(pair, 0), wider(get(pair, 1))))
    total = (pick(head, none, total[0]), total[1])
    put_map(mine, total)

    @pl.when(role == 0)
    def _():
        pl.semaphore_wait(met.at[1], 1)

    def neighbour(d, whole_map):
        part = pl.ds(0, 3 * width + 16) if whole_map else constant
        return remote(mine.at[part], slots.at[d - 1, part], me + stride * d, 2 + d, 2 + d)

    def for_kinds(d, sender, act):
        test = spot + d < group if sender else spot >= d
        at_head = head if sender else place == d
        pl.when(jnp.logical_and(test, at_head))(lambda: act(neighbour(d, False)))
        pl.when(jnp.logical_and(test, jnp.logical_not(at_head)))(lambda: act(neighbour(d, True)))

    for d in reversed(range(1, group)):
        for_kinds(d, True, lambda copy: copy.start())

    g = blocks()[0]
    up, down = upward(), downward()[::-1]
    up_part, down_part = [up[0]], [down[0]]
    for i in range(1, layers):
        up_part.append(merged(up_part[-1], up[i]))
        if i + 1 < layers:
            down_part.append(merged(down_part[-1], down[i]))
    for i in range(layers):
        m_part, s_part = up_part[i]
        put(factors, m_part, role, i)
        if i + 1 < layers:
            m_rest, s_rest = down_part[layers - 2 - i]
            put(factors, product(g[i], m_rest), 1 - role, i)
            put(base, plus(s_part, sandwich(g[i], s_rest)), i)
        else:
            put(factors, g[i], 1 - role, i)
            put(base, s_part, i)
    hint.wait_recv()
    for i in range(layers):
        factor = get(factors, 1, i)
        put(base, plus(get(base, i), sandwich(factor, get(given, 1))), i)
        put(factors, product(factor, get(given, 0)), 1, i)

    for d in reversed(range(1, group)):
        for_kinds(d, False, lambda copy: copy.wait_recv())
    arrived = [get_map(slots, d - 1) for d in reversed(range(1, group))]
    if arrived:
        lower = arrived[:-1] and [whole(arrived[:-1])]
        before = whole(lower + arrived[-1:])
        total = whole(lower + [merged(arrived[-1], total)])
    else:
        before = ((square, zeros), wider(none))
    before = (pick(head, none, before[0]), pick(head, wider(start), before[1]))

    def deliveries(k, whole_map):
        part = pl.ds(0, 3 * width + 16) if whole_map else constant
        at = 2 + group + 2 ** k - 2**near
        return [
            remote(relay.at[k - near, part], inbox.at[k - near, part], me + stride * (1 + d), at + d, 2 + group + k - near)
            for d in range(2**k)
        ]

    for k in middle:

        @pl.when(gives[k])
        def _():
            put_map(relay, total, k - near)

        for whole_map in (False, True):

            @pl.when(jnp.logical_and(gives[k], (lows[k] != 0) == whole_map))
            def _():
                for copy in reversed(deliveries(k, whole_map)):
                    copy.start()

            @pl.when(jnp.logical_and(takes[k], (lows[k] != 0) == whole_map))
            def _():
                deliveries(k, whole_map)[0].wait_recv()

        got = get_map(inbox, k - near)
        total = merged(got, total)
        before = merged(got, before)

    last = 2 + group + half - 2**near
    last_recv = 2 + group + len(middle)

    def final(d, twin):
        other = me + stride * (1 + d)
        other = other + 1 - 2 * role if twin else other
        return remote(post, late, other, last + 2 * d + twin, last_recv)

    @pl.when(gives_last)
    def _():
        put_packed(post, total[1], 0)
        for d in reversed(range(half)):
            final(d, 0).start()
            final(d, 1).start()

    put(ends, before[0], 0, 0)
    put(ends, before[1], 0, 1)
    share = remote(ends.at[0], ends.at[1], mate, 2, 2)
    share.start()

    def add(k):
        rows = jnp.concatenate([wide(get(factors, k, i)) for i in range(layers)], axis=0)
        inner = times(rows, get(ends, k, 1)).astype(BF)
        for i in range(layers):
            term = halves(times_transpose(inner[i * width : (i + 1) * width], get(factors, k, i)))
            put(base, plus(get(base, i), term), i)

    add(0)
    share.wait_recv()
    add(1)
    edge = get(ends, slow, 0)
    rows = jnp.concatenate([wide(get(factors, slow, i)) for i in range(layers)], axis=0)
    rows = times(rows, edge).astype(BF)
    final(0, 0).wait_recv()
    state = low(get_packed(late, 0))
    inner = times(rows, state).astype(BF)
    for i in range(layers):
        part = slice(i * width, (i + 1) * width)
        value = plus(get(base, i), halves(times_transpose(inner[part], halves(rows[part]))))
        out[0, i] = value[0]
        out[1, i] = value[1]

    swap.wait_send()
    hint.wait_send()
    share.wait_send()
    for d in range(1, group):
        for_kinds(d, True, lambda copy: copy.wait_send())
    for k in middle:
        for whole_map in (False, True):

            @pl.when(jnp.logical_and(gives[k], (lows[k] != 0) == whole_map))
            def _():
                for copy in deliveries(k, whole_map):
                    copy.wait_send()

    @pl.when(gives_last)
    def _():
        for d in range(half):
            final(d, 0).wait_send()
            final(d, 1).wait_send()


def solution(mesh):
    peers = mesh.shape["slab"]
    bits = (peers // 2).bit_length() - 1
    near = min(2, bits - 1)
    group, half, hops = 2**near, 2 ** (bits - 1), bits - 1 - near

    def local(slab_green, coupling, left_lead_surface, sigma_right):
        layers, width = slab_green.shape[1], slab_green.shape[2]
        vmem = pl.BlockSpec(memory_space=pltpu.VMEM)
        block = (2, width, width)
        packed, chart = (width + 16, width), (3 * width + 16, width)
        return pl.pallas_call(
            functools.partial(kernel, bits, near),
            out_shape=jax.ShapeDtypeStruct(slab_green.shape, F32),
            in_specs=[pl.BlockSpec(memory_space=pltpu.HBM)] * 4,
            out_specs=vmem,
            scratch_shapes=[
                pltpu.VMEM(slab_green.shape, BF),
                pltpu.VMEM(coupling.shape, BF),
                pltpu.VMEM(block, BF),
                pltpu.VMEM(block, BF),
                pltpu.VMEM((2, 2, *block), BF),
                pltpu.VMEM((2, *block), BF),
                pltpu.VMEM((2, *block), BF),
                pltpu.VMEM((2, layers, *block), BF),
                pltpu.VMEM((layers, *block), F32),
                pltpu.VMEM(chart, BF),
                pltpu.VMEM((max(group - 1, 1), *chart), BF),
                pltpu.VMEM((max(hops, 1), *chart), BF),
                pltpu.VMEM((max(hops, 1), *chart), BF),
                pltpu.VMEM((2, 2, *block), BF),
                pltpu.VMEM(packed, BF),
                pltpu.VMEM(packed, BF),
                pltpu.SemaphoreType.DMA((2 + group + half - group + 2 * half,)),
                pltpu.SemaphoreType.DMA((3 + group + hops,)),
                pltpu.SemaphoreType.DMA((4,)),
                pltpu.SemaphoreType.REGULAR((2,)),
            ],
            compiler_params=pltpu.CompilerParams(collective_id=0, has_side_effects=True, vmem_limit_bytes=16777216),
        )(*[pltpu.with_memory_space_constraint(a, pltpu.HBM) for a in (slab_green, coupling, left_lead_surface, sigma_right)])

    in_specs = (
        P(None, ("energy", "slab"), None, None),
        P(None, ("energy", "slab"), None, None),
        P("energy", None, None),
        P("energy", None, None),
    )
    out_specs = P(None, ("energy", "slab"), None, None)
    return jax.shard_map(local, mesh=mesh, in_specs=in_specs, out_specs=out_specs, check_vma=False)
```

```python
import functools

import jax
import jax.numpy as jnp
from jax import lax
from jax.experimental import pallas as pl
from jax.experimental.pallas import tpu as pltpu
from jax.sharding import PartitionSpec as P

MESH = pl.DeviceIdType.MESH
BF = jnp.bfloat16
F32 = jnp.float32


def wide(value):
    return jnp.concatenate([value[0], value[1]], axis=1)


def halves(out):
    width = out.shape[1] // 2
    return out[:, :width], out[:, width:]


def low(value):
    return value[0].astype(BF), value[1].astype(BF)


def plus(a, b):
    return a[0] + b[0], a[1] + b[1]


def times(rows, right):
    weights = jnp.concatenate(
        [wide(right), jnp.concatenate([-right[1], right[0]], axis=1)], axis=0
    )
    return jnp.dot(rows, weights, preferred_element_type=F32)


def times_transpose(rows, right):
    weights = jnp.concatenate(
        [
            jnp.concatenate([right[0], -right[1]], axis=1),
            jnp.concatenate([right[1], right[0]], axis=1),
        ],
        axis=0,
    )
    return lax.dot_general(rows, weights, (((1,), (1,)), ((), ())), preferred_element_type=F32)


def product(a, b):
    return low(halves(times(wide(a), b)))


def sandwich(factor, middle):
    inner = times(wide(factor), low(middle)).astype(BF)
    return halves(times_transpose(inner, factor))


def get(ref, *index):
    return ref[(*index, 0)], ref[(*index, 1)]


def put(ref, value, *index):
    ref[(*index, 0)] = value[0].astype(ref.dtype)
    ref[(*index, 1)] = value[1].astype(ref.dtype)


def kernel(
    bits,
    near,
    green_hbm,
    link_hbm,
    lead_hbm,
    sigma_hbm,
    out,
    green,
    link,
    lead,
    sigma,
    own,
    pair,
    given,
    factors,
    base,
    slots,
    relay,
    inbox,
    ends,
    post,
    late,
    send_sem,
    recv_sem,
    load_sem,
    met,
):
    loads = [
        pltpu.make_async_copy(source, target, load_sem.at[k])
        for k, (source, target) in enumerate(
            [(green_hbm, green), (link_hbm, link), (lead_hbm, lead), (sigma_hbm, sigma)]
        )
    ]
    for load in loads:
        load.start()
    layers, width = green.shape[1], green.shape[2]
    energy, me = lax.axis_index("energy"), lax.axis_index("slab")
    role, chip = me % 2, me // 2
    mate = me + 1 - 2 * role
    chips, half, group = 2**bits, 2 ** (bits - 1), 2**near
    duo = min(2, group)
    place = chip + role * (chips - 1 - 2 * chip)
    stride = (1 - 2 * role) * 2
    spot = place % group
    head = place == 0
    middle = range(near, bits - 1)
    lows = {k: place // 2 ** (k + 1) * 2 ** (k + 1) for k in middle}
    gives = {k: place == lows[k] + 2**k - 1 for k in middle}
    takes = {k: (place // 2**k) % 2 == 1 for k in middle}
    gives_last = place // duo == half // duo - 1
    upper = chip // half
    there = half - duo + jnp.where(upper == 1, chip, chips - 1 - chip) % duo
    giver = jnp.where(upper == 1, there, chips - 1 - there) * 2
    slow = (1 - upper + role) % 2

    barrier = pltpu.get_barrier_semaphore()

    def greet(other):
        pl.semaphore_signal(barrier, inc=1, device_id=(energy, other), device_id_type=MESH)

    def far_greet(other):
        greet(other // 2 * 2 + 1)

    def receivers(place):
        found = group - 1 - place % group + jnp.where(place // duo == half // duo - 1, 2 * (half // duo), 0)
        if duo > 1:
            found = found + jnp.where(place % group == group - 1, 1, 0)
        for k in middle:
            found = found + jnp.where(place % 2 ** (k + 1) == 2**k - 1, 2**k, 0)
        return found

    def sources():
        for p in range(group):
            test = p < spot
            if duo > 1 and p == group - 1:
                test = spot == group - 2
            yield p, test, place - spot + p == 0

    for p, test, _ in sources():

        @pl.when(test)
        def _():
            far_greet(me + stride * (p - spot))

    for k in middle:

        @pl.when(takes[k])
        def _():
            far_greet(me + stride * (lows[k] + 2**k - 1 - place))

    far_greet(giver)

    def tell(at):
        pl.semaphore_signal(met.at[at], inc=1, device_id=(energy, mate), device_id_type=MESH)

    @pl.when(role == 1)
    def _():
        greet(mate)

    @pl.when(role == 0)
    def _():
        pl.semaphore_wait(barrier, 1)
        tell(0)

    def remote(source, target, other, sender, receiver):
        return pltpu.make_async_remote_copy(
            src_ref=source,
            dst_ref=target,
            send_sem=send_sem.at[sender],
            recv_sem=recv_sem.at[receiver],
            device_id=(energy, other),
            device_id_type=MESH,
        )

    row = lax.broadcasted_iota(jnp.int32, (width, width), 0)
    column = lax.broadcasted_iota(jnp.int32, (width, width), 1)
    zeros = jnp.zeros((width, width), BF)
    square = jnp.where(row == column, 1.0, 0.0).astype(BF)
    none = (zeros, zeros)
    linear, constant = pl.ds(0, 2 * width), pl.ds(2 * width, width + 16)

    def wider(value):
        return value[0].astype(F32), value[1].astype(F32)

    def pick(test, a, b):
        return jnp.where(test, a[0], b[0]), jnp.where(test, a[1], b[1])

    def put_linear(ref, value, *index):
        ref[(*index, pl.ds(0, width))] = value[0]
        ref[(*index, pl.ds(width, width))] = value[1]

    def put_packed(ref, value, at, *index):
        ref[(*index, pl.ds(at, width))] = jnp.where(row <= column, value[0], value[1]).astype(BF)
        diagonal = jnp.sum(jnp.where(row == column, value[1], 0.0), axis=0, keepdims=True)
        ref[(*index, pl.ds(at + width, 16))] = jnp.broadcast_to(diagonal, (16, width)).astype(BF)

    def get_packed(ref, at, *index):
        mixed = ref[(*index, pl.ds(at, width))]
        flipped = mixed.T.astype(F32)
        mixed = mixed.astype(F32)
        diagonal = ref[(*index, pl.ds(at + width, 16))].astype(F32)[0:1]
        return (
            jnp.where(row <= column, mixed, flipped),
            jnp.where(row > column, mixed, jnp.where(row == column, diagonal, flipped)),
        )

    def get_map(ref, *index):
        first = (ref[(*index, pl.ds(0, width))], ref[(*index, pl.ds(width, width))])
        return first, get_packed(ref, 2 * width, *index)

    def put_map(ref, value, *index):
        put_linear(ref, value[0], *index)
        put_packed(ref, value[1], 2 * width, *index)

    blank = jnp.zeros((width + 16, width), BF)
    for p, test, first in sources():

        @pl.when(jnp.logical_not(jnp.logical_or(test, spot == p)))
        def _():
            put_linear(slots, (square, zeros), p)
            slots[p, constant] = blank

        @pl.when(jnp.logical_and(test, first))
        def _():
            put_linear(slots, none, p)

    for k in middle:

        @pl.when(jnp.logical_not(takes[k]))
        def _():
            put_linear(inbox, (square, zeros), k - near)
            inbox[k - near, constant] = blank

        @pl.when(jnp.logical_and(takes[k], lows[k] == 0))
        def _():
            put_linear(inbox, none, k - near)

    for load in loads[:2]:
        load.wait()

    def merged(first, second):
        return (
            product(second[0], first[0]),
            plus(sandwich(second[0], first[1]), second[1]),
        )

    def whole(items):
        while len(items) > 1:
            rest = items[len(items) // 2 * 2 :]
            items = [merged(*items[k : k + 2]) for k in range(0, len(items) - 1, 2)] + rest
        return items[0]

    def blocks():
        return (
            [(green[0, i], green[1, i]) for i in range(layers)],
            [(link[0, i], link[1, i]) for i in range(layers)],
        )

    def upward():
        g, c = blocks()
        return [(low(halves(times_transpose(wide(g[i]), c[i]))), g[i]) for i in range(layers)]

    def downward():
        g, c = blocks()
        back = [product(c[i], g[i]) for i in range(layers)]
        return [(back[i], halves(times_transpose(wide(back[i]), c[i]))) for i in range(layers)]

    def keep(at, value):
        put(own, value[0], at, 0)
        put(own, value[1], at, 1)

    def neighbour(source, target, whole_map):
        part = pl.ds(0, 3 * width + 16) if whole_map else constant
        return remote(
            slots.at[source, part], slots.at[source, part], me + stride * (target - spot), 3 + target, 3 + source
        )

    def by_kind(test, first, source, target, act):
        pl.when(jnp.logical_and(test, first))(lambda: act(neighbour(source, target, False)))
        pl.when(jnp.logical_and(test, jnp.logical_not(first)))(lambda: act(neighbour(source, target, True)))

    def for_targets(act):
        for p in reversed(range(group)):
            test = spot < p
            if duo > 1 and p == group - 2:
                test = jnp.logical_or(test, spot == group - 1)
            by_kind(test, head, spot, p, act)

    forward = role == 0
    swap = remote(own.at[1], pair, mate, 0, 0)

    def advance():
        start = (
            jnp.where(forward, lead[0], sigma[0]),
            jnp.where(forward, lead[1], sigma[1]),
        )
        first = (get(own, 0, 0), wider(get(own, 0, 1)))
        first = (first[0], pick(head, plus(sandwich(first[0], start), first[1]), first[1]))
        swap.wait_recv()
        total = merged(first, (get(pair, 0), wider(get(pair, 1))))
        put_map(slots, (pick(head, none, total[0]), total[1]), spot)

    keep(1 - role, whole(downward()[::-1]))
    for load in loads[2:]:
        load.wait()

    @pl.when(role == 1)
    def _():
        pl.semaphore_wait(met.at[0], 1)
        advance()
        pl.semaphore_wait(barrier, receivers(chip) + receivers(chips - 1 - chip))
        tell(1)
        for_targets(lambda copy: copy.start())
        keep(1, whole(upward()))
        swap.start()

    @pl.when(role == 0)
    def _():
        swap.start()
        keep(0, whole(upward()))
        advance()
        pl.semaphore_wait(met.at[1], 1)
        for_targets(lambda copy: copy.start())

    hint = remote(own.at[0], given, mate, 1, 1)
    hint.start()

    g = blocks()[0]
    up, down = upward(), downward()[::-1]
    up_part, down_part = [up[0]], [down[0]]
    for i in range(1, layers):
        up_part.append(merged(up_part[-1], up[i]))
        if i + 1 < layers:
            down_part.append(merged(down_part[-1], down[i]))
    for i in range(layers):
        m_part, s_part = up_part[i]
        put(factors, m_part, role, i)
        if i + 1 < layers:
            m_rest, s_rest = down_part[layers - 2 - i]
            put(factors, product(g[i], m_rest), 1 - role, i)
            put(base, plus(s_part, sandwich(g[i], s_rest)), i)
        else:
            put(factors, g[i], 1 - role, i)
            put(base, s_part, i)
    hint.wait_recv()
    for i in range(layers):
        factor = get(factors, 1, i)
        put(base, plus(get(base, i), sandwich(factor, get(given, 1))), i)
        put(factors, product(factor, get(given, 0)), 1, i)

    for p, test, first in sources():
        by_kind(test, first, p, spot, lambda copy: copy.wait_recv())

    def group_total():
        return whole([get_map(slots, p) for p in range(group)])

    start = (
        jnp.where(forward, lead[0], sigma[0]),
        jnp.where(forward, lead[1], sigma[1]),
    )

    def group_before():
        found = []
        for p in range(group - 1):
            m_part, s_part = get_map(slots, p)
            found.append((pick(p < spot, m_part, (square, zeros)), pick(p < spot, s_part, wider(none))))
        found = whole(found) if found else ((square, zeros), wider(none))
        return pick(head, none, found[0]), pick(head, wider(start), found[1])

    if middle:
        total, before = group_total(), group_before()

    def deliveries(k, whole_map):
        part = pl.ds(0, 3 * width + 16) if whole_map else constant
        at = 3 + 2**k
        return [
            remote(relay.at[k - near, part], inbox.at[k - near, part], me + stride * (1 + d), at + d, 3 + group + k - near)
            for d in range(2**k)
        ]

    for k in middle:

        @pl.when(gives[k])
        def _():
            put_map(relay, total, k - near)

        for whole_map in (False, True):

            @pl.when(jnp.logical_and(gives[k], (lows[k] != 0) == whole_map))
            def _():
                for copy in reversed(deliveries(k, whole_map)):
                    copy.start()

            @pl.when(jnp.logical_and(takes[k], (lows[k] != 0) == whole_map))
            def _():
                deliveries(k, whole_map)[0].wait_recv()

        got = get_map(inbox, k - near)
        total = merged(got, total)
        before = merged(got, before)

    last = 3 + half
    last_recv = 3 + group + len(middle)

    def final(d, core):
        other = (me + stride * duo * (1 + d)) // 2 * 2 + core
        return remote(post, late, other, last + 2 * d + core, last_recv)

    @pl.when(gives_last)
    def _():
        value = total if middle else group_total()
        put_packed(post, value[1], 0)
        for d in reversed(range(half // duo)):
            final(d, 0).start()
            final(d, 1).start()

    if not middle:
        before = group_before()
    put(ends, before[0], 0, 0)
    put(ends, before[1], 0, 1)
    share = remote(ends.at[0], ends.at[1], mate, 2, 2)
    share.start()

    def add(k):
        rows = jnp.concatenate([wide(get(factors, k, i)) for i in range(layers)], axis=0)
        inner = times(rows, get(ends, k, 1)).astype(BF)
        for i in range(layers):
            term = halves(times_transpose(inner[i * width : (i + 1) * width], get(factors, k, i)))
            put(base, plus(get(base, i), term), i)

    add(0)
    share.wait_recv()
    add(1)
    edge = get(ends, slow, 0)
    rows = jnp.concatenate([wide(get(factors, slow, i)) for i in range(layers)], axis=0)
    rows = times(rows, edge).astype(BF)
    final(0, 0).wait_recv()
    state = low(get_packed(late, 0))
    inner = times(rows, state).astype(BF)
    for i in range(layers):
        part = slice(i * width, (i + 1) * width)
        value = plus(get(base, i), halves(times_transpose(inner[part], halves(rows[part]))))
        out[0, i] = value[0]
        out[1, i] = value[1]

    swap.wait_send()
    hint.wait_send()
    share.wait_send()
    for_targets(lambda copy: copy.wait_send())
    for k in middle:
        for whole_map in (False, True):

            @pl.when(jnp.logical_and(gives[k], (lows[k] != 0) == whole_map))
            def _():
                for copy in deliveries(k, whole_map):
                    copy.wait_send()

    @pl.when(gives_last)
    def _():
        for d in range(half // duo):
            final(d, 0).wait_send()
            final(d, 1).wait_send()


def solution(mesh):
    peers = mesh.shape["slab"]
    bits = (peers // 2).bit_length() - 1
    near = min(2, bits - 1)
    group, half, hops = 2**near, 2 ** (bits - 1), bits - 1 - near

    def local(slab_green, coupling, left_lead_surface, sigma_right):
        layers, width = slab_green.shape[1], slab_green.shape[2]
        vmem = pl.BlockSpec(memory_space=pltpu.VMEM)
        block = (2, width, width)
        packed, chart = (width + 16, width), (3 * width + 16, width)
        return pl.pallas_call(
            functools.partial(kernel, bits, near),
            out_shape=jax.ShapeDtypeStruct(slab_green.shape, F32),
            in_specs=[pl.BlockSpec(memory_space=pltpu.HBM)] * 4,
            out_specs=vmem,
            scratch_shapes=[
                pltpu.VMEM(slab_green.shape, BF),
                pltpu.VMEM(coupling.shape, BF),
                pltpu.VMEM(block, BF),
                pltpu.VMEM(block, BF),
                pltpu.VMEM((2, 2, *block), BF),
                pltpu.VMEM((2, *block), BF),
                pltpu.VMEM((2, *block), BF),
                pltpu.VMEM((2, layers, *block), BF),
                pltpu.VMEM((layers, *block), F32),
                pltpu.VMEM((group, *chart), BF),
                pltpu.VMEM((max(hops, 1), *chart), BF),
                pltpu.VMEM((max(hops, 1), *chart), BF),
                pltpu.VMEM((2, 2, *block), BF),
                pltpu.VMEM(packed, BF),
                pltpu.VMEM(packed, BF),
                pltpu.SemaphoreType.DMA((3 + 3 * half,)),
                pltpu.SemaphoreType.DMA((4 + group + hops,)),
                pltpu.SemaphoreType.DMA((4,)),
                pltpu.SemaphoreType.REGULAR((2,)),
            ],
            compiler_params=pltpu.CompilerParams(collective_id=0, has_side_effects=True, vmem_limit_bytes=16777216),
        )(*[pltpu.with_memory_space_constraint(a, pltpu.HBM) for a in (slab_green, coupling, left_lead_surface, sigma_right)])

    in_specs = (
        P(None, ("energy", "slab"), None, None),
        P(None, ("energy", "slab"), None, None),
        P("energy", None, None),
        P("energy", None, None),
    )
    out_specs = P(None, ("energy", "slab"), None, None)
    return jax.shard_map(local, mesh=mesh, in_specs=in_specs, out_specs=out_specs, check_vma=False)
```

```python
import functools

import jax
import jax.numpy as jnp
from jax import lax
from jax.experimental import pallas as pl
from jax.experimental.pallas import tpu as pltpu
from jax.sharding import PartitionSpec as P

MESH = pl.DeviceIdType.MESH
BF = jnp.bfloat16
F32 = jnp.float32


def wide(value):
    return jnp.concatenate([value[0], value[1]], axis=1)


def halves(out):
    width = out.shape[1] // 2
    return out[:, :width], out[:, width:]


def low(value):
    return value[0].astype(BF), value[1].astype(BF)


def plus(a, b):
    return a[0] + b[0], a[1] + b[1]


def times(rows, right):
    weights = jnp.concatenate(
        [wide(right), jnp.concatenate([-right[1], right[0]], axis=1)], axis=0
    )
    return jnp.dot(rows, weights, preferred_element_type=F32)


def times_transpose(rows, right):
    weights = jnp.concatenate(
        [
            jnp.concatenate([right[0], -right[1]], axis=1),
            jnp.concatenate([right[1], right[0]], axis=1),
        ],
        axis=0,
    )
    return lax.dot_general(rows, weights, (((1,), (1,)), ((), ())), preferred_element_type=F32)


def product(a, b):
    return low(halves(times(wide(a), b)))


def sandwich(factor, middle):
    inner = times(wide(factor), low(middle)).astype(BF)
    return halves(times_transpose(inner, factor))


def get(ref, *index):
    return ref[(*index, 0)], ref[(*index, 1)]


def put(ref, value, *index):
    ref[(*index, 0)] = value[0].astype(ref.dtype)
    ref[(*index, 1)] = value[1].astype(ref.dtype)


def kernel(
    bits,
    near,
    green_hbm,
    link_hbm,
    lead_hbm,
    sigma_hbm,
    out,
    green,
    link,
    lead,
    sigma,
    own,
    pair,
    given,
    factors,
    base,
    mine,
    slots,
    relay,
    inbox,
    ends,
    post,
    late,
    send_sem,
    recv_sem,
    load_sem,
    met,
):
    loads = [
        pltpu.make_async_copy(source, target, load_sem.at[k])
        for k, (source, target) in enumerate(
            [(green_hbm, green), (link_hbm, link), (lead_hbm, lead), (sigma_hbm, sigma)]
        )
    ]
    for load in loads:
        load.start()
    layers, width = green.shape[1], green.shape[2]
    energy, me = lax.axis_index("energy"), lax.axis_index("slab")
    role, chip = me % 2, me // 2
    mate = me + 1 - 2 * role
    chips, half, group = 2**bits, 2 ** (bits - 1), 2**near
    place = chip + role * (chips - 1 - 2 * chip)
    stride = (1 - 2 * role) * 2
    spot = place % group
    head = place == 0
    middle = range(near, bits - 1)
    lows = {k: place // 2 ** (k + 1) * 2 ** (k + 1) for k in middle}
    gives = {k: place == lows[k] + 2**k - 1 for k in middle}
    takes = {k: (place // 2**k) % 2 == 1 for k in middle}
    gives_last = place == half - 1
    upper = chip // half
    giver = jnp.where(upper == 1, 2 * (half - 1), 2 * half)
    slow = (1 - upper + role) % 2

    barrier = pltpu.get_barrier_semaphore()

    def greet(other):
        pl.semaphore_signal(barrier, inc=1, device_id=(energy, other), device_id_type=MESH)

    def far_greet(other):
        greet(other // 2 * 2 + 1)

    def receivers(place):
        found = group - 1 - place % group + jnp.where(place == half - 1, 2 * half, 0)
        for k in middle:
            found = found + jnp.where(place % 2 ** (k + 1) == 2**k - 1, 2**k, 0)
        return found

    def sources():
        for p in reversed(range(group - 1)):
            yield p, p < spot, place - spot + p == 0

    for p, test, _ in sources():

        @pl.when(test)
        def _():
            far_greet(me + stride * (p - spot))

    for k in middle:

        @pl.when(takes[k])
        def _():
            far_greet(me + stride * (lows[k] + 2**k - 1 - place))

    far_greet(giver)

    def tell(at):
        pl.semaphore_signal(met.at[at], inc=1, device_id=(energy, mate), device_id_type=MESH)

    @pl.when(role == 1)
    def _():
        greet(mate)

    @pl.when(role == 0)
    def _():
        pl.semaphore_wait(barrier, 1)
        tell(0)

    def remote(source, target, other, sender, receiver):
        return pltpu.make_async_remote_copy(
            src_ref=source,
            dst_ref=target,
            send_sem=send_sem.at[sender],
            recv_sem=recv_sem.at[receiver],
            device_id=(energy, other),
            device_id_type=MESH,
        )

    row = lax.broadcasted_iota(jnp.int32, (width, width), 0)
    column = lax.broadcasted_iota(jnp.int32, (width, width), 1)
    zeros = jnp.zeros((width, width), BF)
    square = jnp.where(row == column, 1.0, 0.0).astype(BF)
    none = (zeros, zeros)
    linear, constant = pl.ds(0, 2 * width), pl.ds(2 * width, width + 16)

    def wider(value):
        return value[0].astype(F32), value[1].astype(F32)

    def pick(test, a, b):
        return jnp.where(test, a[0], b[0]), jnp.where(test, a[1], b[1])

    def put_linear(ref, value, *index):
        ref[(*index, pl.ds(0, width))] = value[0]
        ref[(*index, pl.ds(width, width))] = value[1]

    def put_packed(ref, value, at, *index):
        ref[(*index, pl.ds(at, width))] = jnp.where(row <= column, value[0], value[1]).astype(BF)
        diagonal = jnp.sum(jnp.where(row == column, value[1], 0.0), axis=0, keepdims=True)
        ref[(*index, pl.ds(at + width, 16))] = jnp.broadcast_to(diagonal, (16, width)).astype(BF)

    def get_packed(ref, at, *index):
        mixed = ref[(*index, pl.ds(at, width))]
        flipped = mixed.T.astype(F32)
        mixed = mixed.astype(F32)
        diagonal = ref[(*index, pl.ds(at + width, 16))].astype(F32)[0:1]
        return (
            jnp.where(row <= column, mixed, flipped),
            jnp.where(row > column, mixed, jnp.where(row == column, diagonal, flipped)),
        )

    def get_map(ref, *index):
        first = (ref[(*index, pl.ds(0, width))], ref[(*index, pl.ds(width, width))])
        return first, get_packed(ref, 2 * width, *index)

    def put_map(ref, value, *index):
        put_linear(ref, value[0], *index)
        put_packed(ref, value[1], 2 * width, *index)

    blank = jnp.zeros((width + 16, width), BF)
    for p, test, first in sources():

        @pl.when(jnp.logical_not(test))
        def _():
            put_linear(slots, (square, zeros), p)
            slots[p, constant] = blank

        @pl.when(jnp.logical_and(test, first))
        def _():
            put_linear(slots, none, p)

    for k in middle:

        @pl.when(jnp.logical_not(takes[k]))
        def _():
            put_linear(inbox, (square, zeros), k - near)
            inbox[k - near, constant] = blank

        @pl.when(jnp.logical_and(takes[k], lows[k] == 0))
        def _():
            put_linear(inbox, none, k - near)

    for load in loads[:2]:
        load.wait()

    def merged(first, second):
        return (
            product(second[0], first[0]),
            plus(sandwich(second[0], first[1]), second[1]),
        )

    def whole(items):
        while len(items) > 1:
            rest = items[len(items) // 2 * 2 :]
            items = [merged(*items[k : k + 2]) for k in range(0, len(items) - 1, 2)] + rest
        return items[0]

    def blocks():
        return (
            [(green[0, i], green[1, i]) for i in range(layers)],
            [(link[0, i], link[1, i]) for i in range(layers)],
        )

    def upward():
        g, c = blocks()
        return [(low(halves(times_transpose(wide(g[i]), c[i]))), g[i]) for i in range(layers)]

    def downward():
        g, c = blocks()
        back = [product(c[i], g[i]) for i in range(layers)]
        return [(back[i], halves(times_transpose(wide(back[i]), c[i]))) for i in range(layers)]

    def keep(at, value):
        put(own, value[0], at, 0)
        put(own, value[1], at, 1)

    def neighbour(source, target, whole_map):
        part = pl.ds(0, 3 * width + 16) if whole_map else constant
        other = me + stride * (target - spot)
        return remote(mine.at[part], slots.at[source, part], other, 3 + target, 3 + source)

    def by_kind(test, first, source, target, act):
        pl.when(jnp.logical_and(test, first))(lambda: act(neighbour(source, target, False)))
        pl.when(jnp.logical_and(test, jnp.logical_not(first)))(lambda: act(neighbour(source, target, True)))

    def for_targets(act):
        for p in reversed(range(1, group)):
            by_kind(spot < p, head, spot, p, act)

    forward = role == 0
    swap = remote(own.at[1], pair, mate, 0, 0)

    def advance():
        start = (
            jnp.where(forward, lead[0], sigma[0]),
            jnp.where(forward, lead[1], sigma[1]),
        )
        first = (get(own, 0, 0), wider(get(own, 0, 1)))
        first = (first[0], pick(head, plus(sandwich(first[0], start), first[1]), first[1]))
        swap.wait_recv()
        total = merged(first, (get(pair, 0), wider(get(pair, 1))))
        put_map(mine, (pick(head, none, total[0]), total[1]))

    keep(1 - role, whole(downward()[::-1]))
    for load in loads[2:]:
        load.wait()

    @pl.when(role == 1)
    def _():
        pl.semaphore_wait(met.at[0], 1)
        advance()
        pl.semaphore_wait(barrier, receivers(chip) + receivers(chips - 1 - chip))
        tell(1)
        for_targets(lambda copy: copy.start())
        keep(1, whole(upward()))
        swap.start()

    @pl.when(role == 0)
    def _():
        swap.start()
        keep(0, whole(upward()))
        advance()
        pl.semaphore_wait(met.at[1], 1)
        for_targets(lambda copy: copy.start())

    hint = remote(own.at[0], given, mate, 1, 1)
    hint.start()

    g = blocks()[0]
    up, down = upward(), downward()[::-1]
    up_part, down_part = [up[0]], [down[0]]
    for i in range(1, layers):
        up_part.append(merged(up_part[-1], up[i]))
        if i + 1 < layers:
            down_part.append(merged(down_part[-1], down[i]))
    for i in range(layers):
        m_part, s_part = up_part[i]
        put(factors, m_part, role, i)
        if i + 1 < layers:
            m_rest, s_rest = down_part[layers - 2 - i]
            put(factors, product(g[i], m_rest), 1 - role, i)
            put(base, plus(s_part, sandwich(g[i], s_rest)), i)
        else:
            put(factors, g[i], 1 - role, i)
            put(base, s_part, i)
    hint.wait_recv()
    for i in range(layers):
        factor = get(factors, 1, i)
        put(base, plus(get(base, i), sandwich(factor, get(given, 1))), i)
        put(factors, product(factor, get(given, 0)), 1, i)

    start = (
        jnp.where(forward, lead[0], sigma[0]),
        jnp.where(forward, lead[1], sigma[1]),
    )
    total, before = get_map(mine), []
    for p, test, first in sources():
        by_kind(test, first, p, spot, lambda copy: copy.wait_recv())
        before.insert(0, get_map(slots, p))
        if p == group - 2:
            total = merged(before[0], total)
    if before[:-1]:
        lower = whole(before[:-1])
        total = merged(lower, total)
        before = [lower, before[-1]]
    before.append(((square, zeros), wider(none)))

    def deliveries(k, whole_map):
        part = pl.ds(0, 3 * width + 16) if whole_map else constant
        at = 3 + 2**k
        return [
            remote(relay.at[k - near, part], inbox.at[k - near, part], me + stride * (1 + d), at + d, 3 + group + k - near)
            for d in range(2**k)
        ]

    gots = []
    for k in middle:

        @pl.when(gives[k])
        def _():
            put_map(relay, total, k - near)

        for whole_map in (False, True):

            @pl.when(jnp.logical_and(gives[k], (lows[k] != 0) == whole_map))
            def _():
                for copy in reversed(deliveries(k, whole_map)):
                    copy.start()

            @pl.when(jnp.logical_and(takes[k], (lows[k] != 0) == whole_map))
            def _():
                deliveries(k, whole_map)[0].wait_recv()

        gots.append(get_map(inbox, k - near))
        total = merged(gots[-1], total)

    last = 3 + half
    last_recv = 3 + group + len(middle)

    def final(order, core):
        d = order + role * (half - 1 - 2 * order)
        other = (me + stride * (1 + d)) // 2 * 2 + core
        return remote(post, late, other, last + 2 * order + core, last_recv)

    @pl.when(gives_last)
    def _():
        put_packed(post, total[1], 0)
        for order in range(half):
            final(order, 0).start()
            final(order, 1).start()

    before = whole(before[:2]) if group > 2 else before[0]
    before = (pick(head, none, before[0]), pick(head, wider(start), before[1]))
    for got in gots:
        before = merged(got, before)
    put(ends, before[0], 0, 0)
    put(ends, before[1], 0, 1)
    share = remote(ends.at[0], ends.at[1], mate, 2, 2)
    share.start()

    def add(k):
        rows = jnp.concatenate([wide(get(factors, k, i)) for i in range(layers)], axis=0)
        inner = times(rows, get(ends, k, 1)).astype(BF)
        for i in range(layers):
            term = halves(times_transpose(inner[i * width : (i + 1) * width], get(factors, k, i)))
            put(base, plus(get(base, i), term), i)

    add(0)
    share.wait_recv()
    add(1)
    edge = get(ends, slow, 0)
    rows = jnp.concatenate([wide(get(factors, slow, i)) for i in range(layers)], axis=0)
    rows = times(rows, edge).astype(BF)
    final(0, 0).wait_recv()
    state = low(get_packed(late, 0))
    inner = times(rows, state).astype(BF)
    for i in range(layers):
        part = slice(i * width, (i + 1) * width)
        value = plus(get(base, i), halves(times_transpose(inner[part], halves(rows[part]))))
        out[0, i] = value[0]
        out[1, i] = value[1]

    swap.wait_send()
    hint.wait_send()
    share.wait_send()
    for_targets(lambda copy: copy.wait_send())
    for k in middle:
        for whole_map in (False, True):

            @pl.when(jnp.logical_and(gives[k], (lows[k] != 0) == whole_map))
            def _():
                for copy in deliveries(k, whole_map):
                    copy.wait_send()

    @pl.when(gives_last)
    def _():
        for order in range(half):
            final(order, 0).wait_send()
            final(order, 1).wait_send()


def solution(mesh):
    peers = mesh.shape["slab"]
    bits = (peers // 2).bit_length() - 1
    near = min(2, bits - 1)
    group, half, hops = 2**near, 2 ** (bits - 1), bits - 1 - near

    def local(slab_green, coupling, left_lead_surface, sigma_right):
        layers, width = slab_green.shape[1], slab_green.shape[2]
        vmem = pl.BlockSpec(memory_space=pltpu.VMEM)
        block = (2, width, width)
        packed, chart = (width + 16, width), (3 * width + 16, width)
        return pl.pallas_call(
            functools.partial(kernel, bits, near),
            out_shape=jax.ShapeDtypeStruct(slab_green.shape, F32),
            in_specs=[pl.BlockSpec(memory_space=pltpu.HBM)] * 4,
            out_specs=vmem,
            scratch_shapes=[
                pltpu.VMEM(slab_green.shape, BF),
                pltpu.VMEM(coupling.shape, BF),
                pltpu.VMEM(block, BF),
                pltpu.VMEM(block, BF),
                pltpu.VMEM((2, 2, *block), BF),
                pltpu.VMEM((2, *block), BF),
                pltpu.VMEM((2, *block), BF),
                pltpu.VMEM((2, layers, *block), BF),
                pltpu.VMEM((layers, *block), F32),
                pltpu.VMEM(chart, BF),
                pltpu.VMEM((max(group - 1, 1), *chart), BF),
                pltpu.VMEM((max(hops, 1), *chart), BF),
                pltpu.VMEM((max(hops, 1), *chart), BF),
                pltpu.VMEM((2, 2, *block), BF),
                pltpu.VMEM(packed, BF),
                pltpu.VMEM(packed, BF),
                pltpu.SemaphoreType.DMA((3 + 3 * half,)),
                pltpu.SemaphoreType.DMA((4 + group + hops,)),
                pltpu.SemaphoreType.DMA((4,)),
                pltpu.SemaphoreType.REGULAR((2,)),
            ],
            compiler_params=pltpu.CompilerParams(collective_id=0, has_side_effects=True, vmem_limit_bytes=16777216),
        )(*[pltpu.with_memory_space_constraint(a, pltpu.HBM) for a in (slab_green, coupling, left_lead_surface, sigma_right)])

    in_specs = (
        P(None, ("energy", "slab"), None, None),
        P(None, ("energy", "slab"), None, None),
        P("energy", None, None),
        P("energy", None, None),
    )
    out_specs = P(None, ("energy", "slab"), None, None)
    return jax.shard_map(local, mesh=mesh, in_specs=in_specs, out_specs=out_specs, check_vma=False)
```

```python
import functools

import jax
import jax.numpy as jnp
from jax import lax
from jax.experimental import pallas as pl
from jax.experimental.pallas import tpu as pltpu
from jax.sharding import PartitionSpec as P

MESH = pl.DeviceIdType.MESH
BF = jnp.bfloat16
F32 = jnp.float32


def wide(value):
    return jnp.concatenate([value[0], value[1]], axis=1)


def halves(out):
    width = out.shape[1] // 2
    return out[:, :width], out[:, width:]


def low(value):
    return value[0].astype(BF), value[1].astype(BF)


def plus(a, b):
    return a[0] + b[0], a[1] + b[1]


def times(rows, right):
    weights = jnp.concatenate(
        [wide(right), jnp.concatenate([-right[1], right[0]], axis=1)], axis=0
    )
    return jnp.dot(rows, weights, preferred_element_type=F32)


def times_transpose(rows, right):
    weights = jnp.concatenate(
        [
            jnp.concatenate([right[0], -right[1]], axis=1),
            jnp.concatenate([right[1], right[0]], axis=1),
        ],
        axis=0,
    )
    return lax.dot_general(rows, weights, (((1,), (1,)), ((), ())), preferred_element_type=F32)


def product(a, b):
    return low(halves(times(wide(a), b)))


def sandwich(factor, middle):
    inner = times(wide(factor), low(middle)).astype(BF)
    return halves(times_transpose(inner, factor))


def get(ref, *index):
    return ref[(*index, 0)], ref[(*index, 1)]


def put(ref, value, *index):
    ref[(*index, 0)] = value[0].astype(ref.dtype)
    ref[(*index, 1)] = value[1].astype(ref.dtype)


def kernel(
    bits,
    near,
    green_hbm,
    link_hbm,
    lead_hbm,
    sigma_hbm,
    out,
    green,
    link,
    lead,
    sigma,
    own,
    pair,
    given,
    factors,
    base,
    mine,
    slots,
    relay,
    inbox,
    ends,
    post,
    late,
    send_sem,
    recv_sem,
    load_sem,
    met,
):
    loads = [
        pltpu.make_async_copy(source, target, load_sem.at[k])
        for k, (source, target) in enumerate(
            [(green_hbm, green), (link_hbm, link), (lead_hbm, lead), (sigma_hbm, sigma)]
        )
    ]
    for load in loads:
        load.start()
    layers, width = green.shape[1], green.shape[2]
    energy, me = lax.axis_index("energy"), lax.axis_index("slab")
    role, chip = me % 2, me // 2
    mate = me + 1 - 2 * role
    chips, half, group = 2**bits, 2 ** (bits - 1), 2**near
    place = chip + role * (chips - 1 - 2 * chip)
    stride = (1 - 2 * role) * 2
    spot = place % group
    head = place == 0
    middle = range(near, bits - 1)
    lows = {k: place // 2 ** (k + 1) * 2 ** (k + 1) for k in middle}
    gives = {k: place == lows[k] + 2**k - 1 for k in middle}
    takes = {k: (place // 2**k) % 2 == 1 for k in middle}
    gives_last = place == half - 1
    upper = chip // half
    giver = jnp.where(upper == 1, 2 * (half - 1), 2 * half)
    slow = (1 - upper + role) % 2

    barrier = pltpu.get_barrier_semaphore()

    def greet(other):
        pl.semaphore_signal(barrier, inc=1, device_id=(energy, other), device_id_type=MESH)

    def far_greet(other):
        greet(other // 2 * 2 + 1)

    def receivers(place):
        found = group - 1 - place % group + jnp.where(place == half - 1, 2 * half, 0)
        for k in middle:
            found = found + jnp.where(place % 2 ** (k + 1) == 2**k - 1, 2**k, 0)
        return found

    def sources():
        for p in reversed(range(group - 1)):
            yield p, p < spot, place - spot + p == 0

    for p, test, _ in sources():

        @pl.when(test)
        def _():
            far_greet(me + stride * (p - spot))

    for k in middle:

        @pl.when(takes[k])
        def _():
            far_greet(me + stride * (lows[k] + 2**k - 1 - place))

    far_greet(giver)

    def tell(at):
        pl.semaphore_signal(met.at[at], inc=1, device_id=(energy, mate), device_id_type=MESH)

    @pl.when(role == 1)
    def _():
        greet(mate)

    @pl.when(role == 0)
    def _():
        pl.semaphore_wait(barrier, 1)
        tell(0)

    def remote(source, target, other, sender, receiver):
        return pltpu.make_async_remote_copy(
            src_ref=source,
            dst_ref=target,
            send_sem=send_sem.at[sender],
            recv_sem=recv_sem.at[receiver],
            device_id=(energy, other),
            device_id_type=MESH,
        )

    row = lax.broadcasted_iota(jnp.int32, (width, width), 0)
    column = lax.broadcasted_iota(jnp.int32, (width, width), 1)
    zeros = jnp.zeros((width, width), BF)
    square = jnp.where(row == column, 1.0, 0.0).astype(BF)
    none = (zeros, zeros)
    linear, constant = pl.ds(0, 2 * width), pl.ds(2 * width, width + 16)

    def wider(value):
        return value[0].astype(F32), value[1].astype(F32)

    def pick(test, a, b):
        return jnp.where(test, a[0], b[0]), jnp.where(test, a[1], b[1])

    def put_linear(ref, value, *index):
        ref[(*index, pl.ds(0, width))] = value[0]
        ref[(*index, pl.ds(width, width))] = value[1]

    def put_packed(ref, value, at, *index):
        ref[(*index, pl.ds(at, width))] = jnp.where(row <= column, value[0], value[1]).astype(BF)
        diagonal = jnp.sum(jnp.where(row == column, value[1], 0.0), axis=0, keepdims=True)
        ref[(*index, pl.ds(at + width, 16))] = jnp.broadcast_to(diagonal, (16, width)).astype(BF)

    def get_packed(ref, at, *index):
        mixed = ref[(*index, pl.ds(at, width))]
        flipped = mixed.T.astype(F32)
        mixed = mixed.astype(F32)
        diagonal = ref[(*index, pl.ds(at + width, 16))].astype(F32)[0:1]
        return (
            jnp.where(row <= column, mixed, flipped),
            jnp.where(row > column, mixed, jnp.where(row == column, diagonal, flipped)),
        )

    def get_map(ref, *index):
        first = (ref[(*index, pl.ds(0, width))], ref[(*index, pl.ds(width, width))])
        return first, get_packed(ref, 2 * width, *index)

    def put_map(ref, value, *index):
        put_linear(ref, value[0], *index)
        put_packed(ref, value[1], 2 * width, *index)

    blank = jnp.zeros((width + 16, width), BF)
    for p, test, first in sources():

        @pl.when(jnp.logical_not(test))
        def _():
            put_linear(slots, (square, zeros), p)
            slots[p, constant] = blank

        @pl.when(jnp.logical_and(test, first))
        def _():
            put_linear(slots, none, p)

    for k in middle:

        @pl.when(jnp.logical_not(takes[k]))
        def _():
            put_linear(inbox, (square, zeros), k - near)
            inbox[k - near, constant] = blank

        @pl.when(jnp.logical_and(takes[k], lows[k] == 0))
        def _():
            put_linear(inbox, none, k - near)

    for load in loads[:2]:
        load.wait()

    def merged(first, second):
        return (
            product(second[0], first[0]),
            plus(sandwich(second[0], first[1]), second[1]),
        )

    def whole(items):
        while len(items) > 1:
            rest = items[len(items) // 2 * 2 :]
            items = [merged(*items[k : k + 2]) for k in range(0, len(items) - 1, 2)] + rest
        return items[0]

    def blocks():
        return (
            [(green[0, i], green[1, i]) for i in range(layers)],
            [(link[0, i], link[1, i]) for i in range(layers)],
        )

    def upward():
        g, c = blocks()
        return [(low(halves(times_transpose(wide(g[i]), c[i]))), g[i]) for i in range(layers)]

    def downward():
        g, c = blocks()
        back = [product(c[i], g[i]) for i in range(layers)]
        return [(back[i], halves(times_transpose(wide(back[i]), c[i]))) for i in range(layers)]

    def keep(at, value):
        put(own, value[0], at, 0)
        put(own, value[1], at, 1)

    def neighbour(source, target, whole_map):
        part = pl.ds(0, 3 * width + 16) if whole_map else constant
        other = me + stride * (target - spot)
        return remote(mine.at[part], slots.at[source, part], other, 3 + target, 3 + source)

    def by_kind(test, first, source, target, act):
        pl.when(jnp.logical_and(test, first))(lambda: act(neighbour(source, target, False)))
        pl.when(jnp.logical_and(test, jnp.logical_not(first)))(lambda: act(neighbour(source, target, True)))

    def for_targets(act):
        for p in reversed(range(1, group)):
            by_kind(spot < p, head, spot, p, act)

    forward = role == 0
    swap = remote(own.at[1], pair, mate, 0, 0)

    def advance():
        start = (
            jnp.where(forward, lead[0], sigma[0]),
            jnp.where(forward, lead[1], sigma[1]),
        )
        first = (get(own, 0, 0), wider(get(own, 0, 1)))
        first = (first[0], pick(head, plus(sandwich(first[0], start), first[1]), first[1]))
        swap.wait_recv()
        total = merged(first, (get(pair, 0), wider(get(pair, 1))))
        put_map(mine, (pick(head, none, total[0]), total[1]))

    def find(at, first):
        pl.when((upper == 1) == first)(lambda: keep(at, whole(downward()[::-1])))
        pl.when((upper == 0) == first)(lambda: keep(at, whole(upward())))

    def gather():
        @pl.when(role == 1)
        def _():
            pl.semaphore_wait(barrier, receivers(chip) + receivers(chips - 1 - chip))
            tell(1)

    def dispatch():
        @pl.when(role == 0)
        def _():
            pl.semaphore_wait(met.at[1], 1)

        for_targets(lambda copy: copy.start())

    find((role + upper) % 2, True)
    for load in loads[2:]:
        load.wait()

    @pl.when(role == 1)
    def _():
        pl.semaphore_wait(met.at[0], 1)

    @pl.when(role == upper)
    def _():
        advance()
        gather()
        dispatch()
        find(1, False)
        swap.start()

    @pl.when(role != upper)
    def _():
        swap.start()
        find(0, False)
        gather()
        advance()
        dispatch()

    hint = remote(own.at[0], given, mate, 1, 1)
    hint.start()

    g = blocks()[0]
    up, down = upward(), downward()[::-1]
    up_part, down_part = [up[0]], [down[0]]
    for i in range(1, layers):
        up_part.append(merged(up_part[-1], up[i]))
        if i + 1 < layers:
            down_part.append(merged(down_part[-1], down[i]))
    for i in range(layers):
        m_part, s_part = up_part[i]
        put(factors, m_part, role, i)
        if i + 1 < layers:
            m_rest, s_rest = down_part[layers - 2 - i]
            put(factors, product(g[i], m_rest), 1 - role, i)
            put(base, plus(s_part, sandwich(g[i], s_rest)), i)
        else:
            put(factors, g[i], 1 - role, i)
            put(base, s_part, i)
    start = (
        jnp.where(forward, lead[0], sigma[0]),
        jnp.where(forward, lead[1], sigma[1]),
    )
    total, before = get_map(mine), []
    for p, test, first in sources():
        by_kind(test, first, p, spot, lambda copy: copy.wait_recv())
    before = [get_map(slots, p) for p in range(group - 1)]
    if before:
        total = merged(before[-1], total)
    if before[:-1]:
        lower = whole(before[:-1])
        total = merged(lower, total)
        before = [lower, before[-1]]
    before.append(((square, zeros), wider(none)))

    def deliveries(k, whole_map):
        part = pl.ds(0, 3 * width + 16) if whole_map else constant
        at = 3 + 2**k
        return [
            remote(relay.at[k - near, part], inbox.at[k - near, part], me + stride * (1 + d), at + d, 3 + group + k - near)
            for d in range(2**k)
        ]

    gots = []
    for k in middle:

        @pl.when(gives[k])
        def _():
            put_map(relay, total, k - near)

        for whole_map in (False, True):

            @pl.when(jnp.logical_and(gives[k], (lows[k] != 0) == whole_map))
            def _():
                for copy in reversed(deliveries(k, whole_map)):
                    copy.start()

            @pl.when(jnp.logical_and(takes[k], (lows[k] != 0) == whole_map))
            def _():
                deliveries(k, whole_map)[0].wait_recv()

        gots.append(get_map(inbox, k - near))
        total = merged(gots[-1], total)

    last = 3 + half
    last_recv = 3 + group + len(middle)

    def final(order, core):
        d = order + role * (half - 1 - 2 * order)
        other = (me + stride * (1 + d)) // 2 * 2 + core
        return remote(post, late, other, last + 2 * order + core, last_recv)

    @pl.when(gives_last)
    def _():
        put_packed(post, total[1], 0)
        for order in range(half):
            final(order, 0).start()
            final(order, 1).start()

    before = whole(before[:2]) if group > 2 else before[0]
    before = (pick(head, none, before[0]), pick(head, wider(start), before[1]))
    for got in gots:
        before = merged(got, before)
    put(ends, before[0], 0, 0)
    put(ends, before[1], 0, 1)
    share = remote(ends.at[0], ends.at[1], mate, 2, 2)
    share.start()
    hint.wait_recv()
    for i in range(layers):
        factor = get(factors, 1, i)
        put(base, plus(get(base, i), sandwich(factor, get(given, 1))), i)
        put(factors, product(factor, get(given, 0)), 1, i)

    def add(k):
        rows = jnp.concatenate([wide(get(factors, k, i)) for i in range(layers)], axis=0)
        inner = times(rows, get(ends, k, 1)).astype(BF)
        for i in range(layers):
            term = halves(times_transpose(inner[i * width : (i + 1) * width], get(factors, k, i)))
            put(base, plus(get(base, i), term), i)

    add(0)
    share.wait_recv()
    add(1)
    edge = get(ends, slow, 0)
    rows = jnp.concatenate([wide(get(factors, slow, i)) for i in range(layers)], axis=0)
    rows = times(rows, edge).astype(BF)
    final(0, 0).wait_recv()
    state = low(get_packed(late, 0))
    inner = times(rows, state).astype(BF)
    for i in range(layers):
        part = slice(i * width, (i + 1) * width)
        value = plus(get(base, i), halves(times_transpose(inner[part], halves(rows[part]))))
        out[0, i] = value[0]
        out[1, i] = value[1]

    swap.wait_send()
    hint.wait_send()
    share.wait_send()
    for_targets(lambda copy: copy.wait_send())
    for k in middle:
        for whole_map in (False, True):

            @pl.when(jnp.logical_and(gives[k], (lows[k] != 0) == whole_map))
            def _():
                for copy in deliveries(k, whole_map):
                    copy.wait_send()

    @pl.when(gives_last)
    def _():
        for order in range(half):
            final(order, 0).wait_send()
            final(order, 1).wait_send()


def solution(mesh):
    peers = mesh.shape["slab"]
    bits = (peers // 2).bit_length() - 1
    near = min(2, bits - 1)
    group, half, hops = 2**near, 2 ** (bits - 1), bits - 1 - near

    def local(slab_green, coupling, left_lead_surface, sigma_right):
        layers, width = slab_green.shape[1], slab_green.shape[2]
        vmem = pl.BlockSpec(memory_space=pltpu.VMEM)
        block = (2, width, width)
        packed, chart = (width + 16, width), (3 * width + 16, width)
        return pl.pallas_call(
            functools.partial(kernel, bits, near),
            out_shape=jax.ShapeDtypeStruct(slab_green.shape, F32),
            in_specs=[pl.BlockSpec(memory_space=pltpu.HBM)] * 4,
            out_specs=vmem,
            scratch_shapes=[
                pltpu.VMEM(slab_green.shape, BF),
                pltpu.VMEM(coupling.shape, BF),
                pltpu.VMEM(block, BF),
                pltpu.VMEM(block, BF),
                pltpu.VMEM((2, 2, *block), BF),
                pltpu.VMEM((2, *block), BF),
                pltpu.VMEM((2, *block), BF),
                pltpu.VMEM((2, layers, *block), BF),
                pltpu.VMEM((layers, *block), F32),
                pltpu.VMEM(chart, BF),
                pltpu.VMEM((max(group - 1, 1), *chart), BF),
                pltpu.VMEM((max(hops, 1), *chart), BF),
                pltpu.VMEM((max(hops, 1), *chart), BF),
                pltpu.VMEM((2, 2, *block), BF),
                pltpu.VMEM(packed, BF),
                pltpu.VMEM(packed, BF),
                pltpu.SemaphoreType.DMA((3 + 3 * half,)),
                pltpu.SemaphoreType.DMA((4 + group + hops,)),
                pltpu.SemaphoreType.DMA((4,)),
                pltpu.SemaphoreType.REGULAR((2,)),
            ],
            compiler_params=pltpu.CompilerParams(collective_id=0, has_side_effects=True, vmem_limit_bytes=16777216),
        )(*[pltpu.with_memory_space_constraint(a, pltpu.HBM) for a in (slab_green, coupling, left_lead_surface, sigma_right)])

    in_specs = (
        P(None, ("energy", "slab"), None, None),
        P(None, ("energy", "slab"), None, None),
        P("energy", None, None),
        P("energy", None, None),
    )
    out_specs = P(None, ("energy", "slab"), None, None)
    return jax.shard_map(local, mesh=mesh, in_specs=in_specs, out_specs=out_specs, check_vma=False)
```

```python
import functools

import jax
import jax.numpy as jnp
from jax import lax
from jax.experimental import pallas as pl
from jax.experimental.pallas import tpu as pltpu
from jax.sharding import PartitionSpec as P

MESH = pl.DeviceIdType.MESH
BF = jnp.bfloat16
F32 = jnp.float32


def wide(value):
    return jnp.concatenate([value[0], value[1]], axis=1)


def halves(out):
    width = out.shape[1] // 2
    return out[:, :width], out[:, width:]


def low(value):
    return value[0].astype(BF), value[1].astype(BF)


def plus(a, b):
    return a[0] + b[0], a[1] + b[1]


def times(rows, right):
    weights = jnp.concatenate(
        [wide(right), jnp.concatenate([-right[1], right[0]], axis=1)], axis=0
    )
    return jnp.dot(rows, weights, preferred_element_type=F32)


def times_transpose(rows, right):
    weights = jnp.concatenate(
        [
            jnp.concatenate([right[0], -right[1]], axis=1),
            jnp.concatenate([right[1], right[0]], axis=1),
        ],
        axis=0,
    )
    return lax.dot_general(rows, weights, (((1,), (1,)), ((), ())), preferred_element_type=F32)


def product(a, b):
    return low(halves(times(wide(a), b)))


def sandwich(factor, middle):
    inner = times(wide(factor), low(middle)).astype(BF)
    return halves(times_transpose(inner, factor))


def get(ref, *index):
    return ref[(*index, 0)], ref[(*index, 1)]


def put(ref, value, *index):
    ref[(*index, 0)] = value[0].astype(ref.dtype)
    ref[(*index, 1)] = value[1].astype(ref.dtype)


def kernel(
    bits,
    near,
    green_hbm,
    link_hbm,
    lead_hbm,
    sigma_hbm,
    out,
    green,
    link,
    lead,
    sigma,
    own,
    pair,
    given,
    factors,
    base,
    mine,
    slots,
    relay,
    inbox,
    ends,
    post,
    late,
    send_sem,
    recv_sem,
    load_sem,
    met,
):
    loads = [
        pltpu.make_async_copy(source, target, load_sem.at[k])
        for k, (source, target) in enumerate(
            [(green_hbm, green), (link_hbm, link), (lead_hbm, lead), (sigma_hbm, sigma)]
        )
    ]
    for load in loads:
        load.start()
    layers, width = green.shape[1], green.shape[2]
    energy, me = lax.axis_index("energy"), lax.axis_index("slab")
    role, chip = me % 2, me // 2
    mate = me + 1 - 2 * role
    chips, half, group = 2**bits, 2 ** (bits - 1), 2**near
    place = chip + role * (chips - 1 - 2 * chip)
    stride = (1 - 2 * role) * 2
    spot = place % group
    head = place == 0
    middle = range(near, bits - 1)
    lows = {k: place // 2 ** (k + 1) * 2 ** (k + 1) for k in middle}
    gives = {k: place == lows[k] + 2**k - 1 for k in middle}
    takes = {k: (place // 2**k) % 2 == 1 for k in middle}
    gives_last = place == half - 1
    upper = chip // half
    giver = jnp.where(upper == 1, 2 * (half - 1), 2 * half)
    slow = (1 - upper + role) % 2

    barrier = pltpu.get_barrier_semaphore()

    def greet(other):
        pl.semaphore_signal(barrier, inc=1, device_id=(energy, other), device_id_type=MESH)

    def far_greet(other):
        greet(other // 2 * 2 + 1)

    def receivers(place):
        found = group - 1 - place % group + jnp.where(place == half - 1, 2 * half, 0)
        for k in middle:
            found = found + jnp.where(place % 2 ** (k + 1) == 2**k - 1, 2**k, 0)
        return found

    def sources():
        for p in reversed(range(group - 1)):
            yield p, p < spot, place - spot + p == 0

    for p, test, _ in sources():

        @pl.when(test)
        def _():
            far_greet(me + stride * (p - spot))

    for k in middle:

        @pl.when(takes[k])
        def _():
            far_greet(me + stride * (lows[k] + 2**k - 1 - place))

    far_greet(giver)

    def tell(at):
        pl.semaphore_signal(met.at[at], inc=1, device_id=(energy, mate), device_id_type=MESH)

    @pl.when(role == 1)
    def _():
        greet(mate)

    @pl.when(role == 0)
    def _():
        pl.semaphore_wait(barrier, 1)
        tell(0)

    def remote(source, target, other, sender, receiver):
        return pltpu.make_async_remote_copy(
            src_ref=source,
            dst_ref=target,
            send_sem=send_sem.at[sender],
            recv_sem=recv_sem.at[receiver],
            device_id=(energy, other),
            device_id_type=MESH,
        )

    row = lax.broadcasted_iota(jnp.int32, (width, width), 0)
    column = lax.broadcasted_iota(jnp.int32, (width, width), 1)
    zeros = jnp.zeros((width, width), BF)
    square = jnp.where(row == column, 1.0, 0.0).astype(BF)
    none = (zeros, zeros)
    linear, constant = pl.ds(0, 2 * width), pl.ds(2 * width, width + 16)

    def wider(value):
        return value[0].astype(F32), value[1].astype(F32)

    def pick(test, a, b):
        return jnp.where(test, a[0], b[0]), jnp.where(test, a[1], b[1])

    def put_linear(ref, value, *index):
        ref[(*index, pl.ds(0, width))] = value[0]
        ref[(*index, pl.ds(width, width))] = value[1]

    def put_packed(ref, value, at, *index):
        ref[(*index, pl.ds(at, width))] = jnp.where(row <= column, value[0], value[1]).astype(BF)
        diagonal = jnp.sum(jnp.where(row == column, value[1], 0.0), axis=0, keepdims=True)
        ref[(*index, pl.ds(at + width, 16))] = jnp.broadcast_to(diagonal, (16, width)).astype(BF)

    def get_packed(ref, at, *index):
        mixed = ref[(*index, pl.ds(at, width))]
        flipped = mixed.T.astype(F32)
        mixed = mixed.astype(F32)
        diagonal = ref[(*index, pl.ds(at + width, 16))].astype(F32)[0:1]
        return (
            jnp.where(row <= column, mixed, flipped),
            jnp.where(row > column, mixed, jnp.where(row == column, diagonal, flipped)),
        )

    def get_map(ref, *index):
        first = (ref[(*index, pl.ds(0, width))], ref[(*index, pl.ds(width, width))])
        return first, get_packed(ref, 2 * width, *index)

    def put_map(ref, value, *index):
        put_linear(ref, value[0], *index)
        put_packed(ref, value[1], 2 * width, *index)

    blank = jnp.zeros((width + 16, width), BF)
    for p, test, first in sources():

        @pl.when(jnp.logical_not(test))
        def _():
            put_linear(slots, (square, zeros), p)
            slots[p, constant] = blank

        @pl.when(jnp.logical_and(test, first))
        def _():
            put_linear(slots, none, p)

    for k in middle:

        @pl.when(jnp.logical_not(takes[k]))
        def _():
            put_linear(inbox, (square, zeros), k - near)
            inbox[k - near, constant] = blank

        @pl.when(jnp.logical_and(takes[k], lows[k] == 0))
        def _():
            put_linear(inbox, none, k - near)

    for load in loads[:2]:
        load.wait()

    def merged(first, second):
        return (
            product(second[0], first[0]),
            plus(sandwich(second[0], first[1]), second[1]),
        )

    def whole(items):
        while len(items) > 1:
            rest = items[len(items) // 2 * 2 :]
            items = [merged(*items[k : k + 2]) for k in range(0, len(items) - 1, 2)] + rest
        return items[0]

    def blocks():
        return (
            [(green[0, i], green[1, i]) for i in range(layers)],
            [(link[0, i], link[1, i]) for i in range(layers)],
        )

    def upward():
        g, c = blocks()
        return [(low(halves(times_transpose(wide(g[i]), c[i]))), g[i]) for i in range(layers)]

    def downward():
        g, c = blocks()
        back = [product(c[i], g[i]) for i in range(layers)]
        return [(back[i], halves(times_transpose(wide(back[i]), c[i]))) for i in range(layers)]

    def keep(at, value):
        put(own, value[0], at, 0)
        put(own, value[1], at, 1)

    def neighbour(source, target, whole_map):
        part = pl.ds(0, 3 * width + 16) if whole_map else constant
        other = me + stride * (target - spot)
        return remote(mine.at[part], slots.at[source, part], other, 3 + target, 3 + source)

    def by_kind(test, first, source, target, act):
        pl.when(jnp.logical_and(test, first))(lambda: act(neighbour(source, target, False)))
        pl.when(jnp.logical_and(test, jnp.logical_not(first)))(lambda: act(neighbour(source, target, True)))

    def for_targets(act):
        for p in reversed(range(1, group)):
            by_kind(spot < p, head, spot, p, act)

    forward = role == 0
    swap = remote(own.at[1], pair, mate, 0, 0)

    def advance():
        start = (
            jnp.where(forward, lead[0], sigma[0]),
            jnp.where(forward, lead[1], sigma[1]),
        )
        first = (get(own, 0, 0), wider(get(own, 0, 1)))
        first = (first[0], pick(head, plus(sandwich(first[0], start), first[1]), first[1]))
        swap.wait_recv()
        total = merged(first, (get(pair, 0), wider(get(pair, 1))))
        put_map(mine, (pick(head, none, total[0]), total[1]))

    def find(at, first):
        pl.when((upper == 1) == first)(lambda: keep(at, whole(downward()[::-1])))
        pl.when((upper == 0) == first)(lambda: keep(at, whole(upward())))

    def gather():
        @pl.when(role == 1)
        def _():
            pl.semaphore_wait(barrier, receivers(chip) + receivers(chips - 1 - chip))
            tell(1)

    def dispatch():
        @pl.when(role == 0)
        def _():
            pl.semaphore_wait(met.at[1], 1)

        for_targets(lambda copy: copy.start())

    find((role + upper) % 2, True)
    for load in loads[2:]:
        load.wait()

    @pl.when(role == 1)
    def _():
        pl.semaphore_wait(met.at[0], 1)

    @pl.when(role == upper)
    def _():
        advance()
        gather()
        dispatch()
        find(1, False)
        swap.start()

    @pl.when(role != upper)
    def _():
        swap.start()
        find(0, False)
        gather()
        advance()
        dispatch()

    hint = remote(own.at[0], given, mate, 1, 1)
    hint.start()

    g = blocks()[0]
    up, down = upward(), downward()[::-1]
    up_part, down_part = [up[0]], [down[0]]
    for i in range(1, layers):
        up_part.append(merged(up_part[-1], up[i]))
        if i + 1 < layers:
            down_part.append(merged(down_part[-1], down[i]))
    for i in range(layers):
        m_part, s_part = up_part[i]
        put(factors, m_part, role, i)
        if i + 1 < layers:
            m_rest, s_rest = down_part[layers - 2 - i]
            put(factors, product(g[i], m_rest), 1 - role, i)
            put(base, plus(s_part, sandwich(g[i], s_rest)), i)
        else:
            put(factors, g[i], 1 - role, i)
            put(base, s_part, i)
    start = (
        jnp.where(forward, lead[0], sigma[0]),
        jnp.where(forward, lead[1], sigma[1]),
    )
    total, before = get_map(mine), []
    for p, test, first in sources():
        by_kind(test, first, p, spot, lambda copy: copy.wait_recv())
    before = [get_map(slots, p) for p in range(group - 1)]
    if before:
        total = merged(before[-1], total)
    if before[:-1]:
        lower = whole(before[:-1])
        total = merged(lower, total)
        before = [lower, before[-1]]
    before.append(((square, zeros), wider(none)))

    def deliveries(k, whole_map):
        part = pl.ds(0, 3 * width + 16) if whole_map else constant
        at = 3 + 2**k
        return [
            remote(relay.at[k - near, part], inbox.at[k - near, part], me + stride * (1 + d), at + d, 3 + group + k - near)
            for d in range(2**k)
        ]

    gots = []
    for k in middle:

        @pl.when(gives[k])
        def _():
            put_map(relay, total, k - near)

        for whole_map in (False, True):

            @pl.when(jnp.logical_and(gives[k], (lows[k] != 0) == whole_map))
            def _():
                for copy in reversed(deliveries(k, whole_map)):
                    copy.start()

            @pl.when(jnp.logical_and(takes[k], (lows[k] != 0) == whole_map))
            def _():
                deliveries(k, whole_map)[0].wait_recv()

        gots.append(get_map(inbox, k - near))
        total = merged(gots[-1], total)

    last = 3 + half
    last_recv = 3 + group + len(middle)

    upward_order = [half // 2] + [d for d in range(half) if d != half // 2]

    def final(order, core):
        d = upward_order[order] + role * (half - 1 - order - upward_order[order])
        other = (me + stride * (1 + d)) // 2 * 2 + core
        return remote(post, late, other, last + 2 * order + core, last_recv)

    @pl.when(gives_last)
    def _():
        put_packed(post, total[1], 0)
        for order in range(half):
            final(order, 0).start()
            final(order, 1).start()

    before = whole(before[:2]) if group > 2 else before[0]
    before = (pick(head, none, before[0]), pick(head, wider(start), before[1]))
    for got in gots:
        before = merged(got, before)
    put(ends, before[0], 0, 0)
    put(ends, before[1], 0, 1)
    share = remote(ends.at[0], ends.at[1], mate, 2, 2)
    share.start()
    hint.wait_recv()
    for i in range(layers):
        factor = get(factors, 1, i)
        put(base, plus(get(base, i), sandwich(factor, get(given, 1))), i)
        put(factors, product(factor, get(given, 0)), 1, i)

    def add(k):
        rows = jnp.concatenate([wide(get(factors, k, i)) for i in range(layers)], axis=0)
        inner = times(rows, get(ends, k, 1)).astype(BF)
        for i in range(layers):
            term = halves(times_transpose(inner[i * width : (i + 1) * width], get(factors, k, i)))
            put(base, plus(get(base, i), term), i)

    add(0)
    share.wait_recv()
    add(1)
    edge = get(ends, slow, 0)
    rows = jnp.concatenate([wide(get(factors, slow, i)) for i in range(layers)], axis=0)
    rows = times(rows, edge).astype(BF)
    final(0, 0).wait_recv()
    state = low(get_packed(late, 0))
    inner = times(rows, state).astype(BF)
    for i in range(layers):
        part = slice(i * width, (i + 1) * width)
        value = plus(get(base, i), halves(times_transpose(inner[part], halves(rows[part]))))
        out[0, i] = value[0]
        out[1, i] = value[1]

    swap.wait_send()
    hint.wait_send()
    share.wait_send()
    for_targets(lambda copy: copy.wait_send())
    for k in middle:
        for whole_map in (False, True):

            @pl.when(jnp.logical_and(gives[k], (lows[k] != 0) == whole_map))
            def _():
                for copy in deliveries(k, whole_map):
                    copy.wait_send()

    @pl.when(gives_last)
    def _():
        for order in range(half):
            final(order, 0).wait_send()
            final(order, 1).wait_send()


def solution(mesh):
    peers = mesh.shape["slab"]
    bits = (peers // 2).bit_length() - 1
    near = min(2, bits - 1)
    group, half, hops = 2**near, 2 ** (bits - 1), bits - 1 - near

    def local(slab_green, coupling, left_lead_surface, sigma_right):
        layers, width = slab_green.shape[1], slab_green.shape[2]
        vmem = pl.BlockSpec(memory_space=pltpu.VMEM)
        block = (2, width, width)
        packed, chart = (width + 16, width), (3 * width + 16, width)
        return pl.pallas_call(
            functools.partial(kernel, bits, near),
            out_shape=jax.ShapeDtypeStruct(slab_green.shape, F32),
            in_specs=[pl.BlockSpec(memory_space=pltpu.HBM)] * 4,
            out_specs=vmem,
            scratch_shapes=[
                pltpu.VMEM(slab_green.shape, BF),
                pltpu.VMEM(coupling.shape, BF),
                pltpu.VMEM(block, BF),
                pltpu.VMEM(block, BF),
                pltpu.VMEM((2, 2, *block), BF),
                pltpu.VMEM((2, *block), BF),
                pltpu.VMEM((2, *block), BF),
                pltpu.VMEM((2, layers, *block), BF),
                pltpu.VMEM((layers, *block), F32),
                pltpu.VMEM(chart, BF),
                pltpu.VMEM((max(group - 1, 1), *chart), BF),
                pltpu.VMEM((max(hops, 1), *chart), BF),
                pltpu.VMEM((max(hops, 1), *chart), BF),
                pltpu.VMEM((2, 2, *block), BF),
                pltpu.VMEM(packed, BF),
                pltpu.VMEM(packed, BF),
                pltpu.SemaphoreType.DMA((3 + 3 * half,)),
                pltpu.SemaphoreType.DMA((4 + group + hops,)),
                pltpu.SemaphoreType.DMA((4,)),
                pltpu.SemaphoreType.REGULAR((2,)),
            ],
            compiler_params=pltpu.CompilerParams(collective_id=0, has_side_effects=True, vmem_limit_bytes=16777216),
        )(*[pltpu.with_memory_space_constraint(a, pltpu.HBM) for a in (slab_green, coupling, left_lead_surface, sigma_right)])

    in_specs = (
        P(None, ("energy", "slab"), None, None),
        P(None, ("energy", "slab"), None, None),
        P("energy", None, None),
        P("energy", None, None),
    )
    out_specs = P(None, ("energy", "slab"), None, None)
    return jax.shard_map(local, mesh=mesh, in_specs=in_specs, out_specs=out_specs, check_vma=False)
```
